128 devices in a mesh: ang: 32 (over z, y, x_hi), pos: 4 (over x_lo, core).
Axes of the slice: x: 4 (x_hi: 2, x_lo: 2; x = x_hi * 2 + x_lo), y: 4, z: 4, core: 2. Of those that a mesh axis runs over, the one named last changes fastest.
Arguments:
- volume: bfloat16 [2, 256, 32768], P(None, 'ang', 'pos'), may hold values from -6 to 6
- radon_tiles: bfloat16 [128, 64, 256], replicated, may hold values from -0.375 to 0.375
- tile_blocks: int32 [128, 32, 4], replicated, may hold values from 0 to 511
- probe_field: bfloat16 [2, 256, 256], replicated, may hold values from -6 to 6
- amplitudes: bfloat16 [128, 16, 256, 256], P('ang', 'pos'), may hold values from 0.099609375 to 3
- offsets: int32 [128, 16], P('ang', 'pos'), may hold values from 0 to 2047, as said below
- counts: int32 [128, 4], P('ang', 'pos'), may hold values from 1 to 4, 12 in all within a row
Outputs:
- new_volume: float32 [2, 256, 32768], P(None, 'ang', 'pos')
- proj_grad: float32 [2, 256, 128, 2048], P(None, None, 'ang', 'pos')
The draws below stay inside these ranges and needn't reach their ends.
Inputs may be any that keep to these rules, and one draw needn't show every extreme that they name: Each position lies in the tile of the device that holds its slot: 512 * (q // 4) <= offsets[a, q] < 512 * (q // 4 + 1). Every row of counts has an entry equal to 4.
All inputs are finite; a program needn't handle non-finite values. No bound on the sum of `counts` on one device may be relied on, other than what follows from the above.
Results may differ from the reference program's by a relative error of at most 0.0062.
Values may be sent and summed in bfloat16 or wider, within the bound.
A program may use at most 192 MiB of HBM per device.

```python
import math
import jax
import jax.numpy as jnp
import numpy as np
from jax import lax

PROBE = 256
U = 2048
BLOCK = 64
J = 4
POS_DEV = 4
ANG = 128
SLICES = 256
TILE_W = 512
UB = 32
KB = 512
KCOEF = 32768
POSITIONS = 16
N_POS = 4


def draw_offsets(key, part):
    slot_index = jnp.arange(POS_DEV * N_POS, dtype=jnp.int32)
    jitter = jax.random.randint(key, (ANG, POS_DEV * N_POS), 0, TILE_W, dtype=jnp.int32)
    jitter = jitter.at[0, 0].set(0)
    jitter = jitter.at[0, POS_DEV * N_POS - 1].set(TILE_W - 1)
    return (slot_index // POS_DEV * TILE_W)[None, :] + jitter


def with_ends(values, stream_key, low, high):
    extent = values.shape
    place = [jax.random.randint(jax.random.fold_in(stream_key, axis), (), 0, extent[axis]) for axis in range(len(extent))]
    values = values.at[tuple(place)].set(low)
    longest = extent.index(max(extent))
    place[longest] = (place[longest] + 1) % extent[longest]
    return values.at[tuple(place)].set(high)


def level_of(rng, dims, pieces, low, top_value):
    def one(dim, blocks):
        heights = jax.random.uniform(jax.random.fold_in(jax.random.fold_in(rng, 6), dim), (blocks,), jnp.float32, low / len(pieces), top_value / len(pieces))
        return jnp.repeat(jnp.exp(heights), dims[dim] // blocks).reshape((-1,) + (1,) * (len(dims) - dim - 1))

    loudness = one(*pieces[0])
    for cut in pieces[1:]:
        loudness = loudness * one(*cut)
    return loudness


def split_up(count, total, reach, lean):
    weights = [(1 << 20) // math.isqrt(grade ** lean) + 1 for grade in range(2, count + 1)]
    surplus, holding = total - reach - (count - 1), [1] * (count - 1)
    while surplus > 0:
        free = [i for i in range(count - 1) if holding[i] < reach]
        whole, remaining = sum([weights[i] for i in free]), surplus
        for i in free:
            extra = min(reach - holding[i], max(1, remaining * weights[i] // whole), surplus)
            holding[i] = holding[i] + extra
            surplus = surplus - extra
    return np.array([reach] + holding)


def uneven_parts(rng, count, total, reach, lean):
    if count == 2:
        one = jax.random.randint(rng, (), max(1, total - reach), min(reach, total - 1) + 1)
        return jnp.stack([one, total - one])
    sizes = jnp.asarray(split_up(count, total, reach, lean), jnp.int32)
    twos = (count - 1) // 2
    donor, taker = sizes[1:1 + 2 * twos:2], sizes[2:2 + 2 * twos:2]
    room = jnp.minimum(donor - 1, reach - taker)
    passed = jax.random.randint(jax.random.fold_in(rng, 1), (twos,), 0, 1 << 20) % (room + 1)
    sizes = sizes.at[1:1 + 2 * twos:2].set(donor - passed).at[2:2 + 2 * twos:2].set(taker + passed)
    return sizes[jax.random.permutation(jax.random.fold_in(rng, 2), count)]


def gaussian(rng, dims, deviation, bound, pieces=(), kind=jnp.bfloat16):
    drawn = deviation * jax.random.normal(rng, dims, jnp.float32)
    if pieces:
        drawn = drawn * level_of(rng, dims, pieces, -0.22, 0.18)
    return jnp.clip(drawn, -bound, bound).astype(kind)


def setup_inputs(seed: int = 0) -> dict:
    splits = jax.random.split(jax.random.key(seed), 8)
    return {
        "volume": gaussian(splits[0], (2, SLICES, KCOEF), 1.0, 6.0, ((1, 32), (2, 4))),
        "radon_tiles": gaussian(splits[1], (ANG, BLOCK, J * BLOCK), (J * BLOCK) ** -0.5, 0.375),
        "tile_blocks": with_ends(jax.random.randint(splits[2], (ANG, UB, J), 0, KB), jax.random.fold_in(splits[2], 1), 0, KB - 1).astype(jnp.int32),
        "probe_field": gaussian(splits[3], (2, PROBE, PROBE), 1.0, 6.0),
        "amplitudes": jnp.clip(jnp.exp(math.log(3.0) - 3.4051113 * jax.random.uniform(splits[4], (ANG, POSITIONS, PROBE, PROBE), jnp.float32) ** level_of(splits[4], (ANG, POSITIONS, PROBE, PROBE), ((0, 32), (1, 4)), -0.2, 0.2)), 0.099609375, 3.0).astype(jnp.bfloat16),
        "offsets": draw_offsets(jax.random.fold_in(splits[7], 71), 0),
        "counts": jax.vmap(lambda own: uneven_parts(own, N_POS, POS_DEV * N_POS * 3 // 4, POS_DEV, 2))(jax.random.split(splits[6], ANG)).reshape((ANG, N_POS)).astype(jnp.int32),
    }


step_size = 0.1

def rounded(value):
    return lax.optimization_barrier(value.astype(jnp.bfloat16))

def dft_tables(width):
    index = jnp.arange(width, dtype=jnp.int32)
    phase = index[:, None] * index[None, :] % width
    turn = 2.0 * math.pi / width * phase.astype(jnp.float32)
    cosine = (jnp.cos(turn) / math.sqrt(width)).astype(jnp.bfloat16)
    sine_neg = (-jnp.sin(turn) / math.sqrt(width)).astype(jnp.bfloat16)
    return (cosine, sine_neg)

def left_mul(table, field):
    return jnp.einsum('zy,qyu->qzu', table.astype(jnp.float32), field.astype(jnp.float32))

def right_mul(field, table):
    return jnp.einsum('qzy,yu->qzu', field.astype(jnp.float32), table.astype(jnp.float32))

def exit_gradient(patches, probe_field, amplitude_rows, live_mask):
    probe_re = probe_field[0].astype(jnp.float32)
    probe_im = probe_field[1].astype(jnp.float32)
    patch_re = patches[:, 0].astype(jnp.float32)
    patch_im = patches[:, 1].astype(jnp.float32)
    wave_re = rounded(probe_re * patch_re - probe_im * patch_im)
    wave_im = rounded(probe_re * patch_im + probe_im * patch_re)
    cosine, sine_neg = dft_tables(patches.shape[-1])
    half_re = rounded(left_mul(cosine, wave_re) - left_mul(sine_neg, wave_im))
    half_im = rounded(left_mul(cosine, wave_im) + left_mul(sine_neg, wave_re))
    far_re = right_mul(half_re, cosine) - right_mul(half_im, sine_neg)
    far_im = right_mul(half_re, sine_neg) + right_mul(half_im, cosine)
    modulus = jnp.sqrt(far_re * far_re + far_im * far_im)
    factor = amplitude_rows.astype(jnp.float32) / jnp.maximum(modulus, 1.0) - 1.0
    delta_re = rounded(far_re * factor)
    delta_im = rounded(far_im * factor)
    back_re = rounded(left_mul(cosine, delta_re) + left_mul(sine_neg, delta_im))
    back_im = rounded(left_mul(cosine, delta_im) - left_mul(sine_neg, delta_re))
    near_re = right_mul(back_re, cosine) + right_mul(back_im, sine_neg)
    near_im = right_mul(back_im, cosine) - right_mul(back_re, sine_neg)
    scale_mask = live_mask[:, None, None]
    grad_re = (probe_re * near_re + probe_im * near_im) * scale_mask
    grad_im = (probe_re * near_im - probe_im * near_re) * scale_mask
    return jnp.stack([grad_re, grad_im], axis=1)

def reference(volume, radon_tiles, tile_blocks, probe_field, amplitudes, offsets, counts):
    blocks = volume.reshape(2, SLICES, KB, BLOCK)

    def forward(pair):
        tile_angle, ids_angle = pair
        picked = jnp.take(blocks, ids_angle.reshape(-1), axis=2)
        picked = picked.reshape(2, SLICES, UB, J * BLOCK)
        products = jnp.einsum('csux,mx->csum', picked.astype(jnp.float32), tile_angle.astype(jnp.float32))
        return products.reshape(2, SLICES, U)
    projection = rounded(lax.map(forward, (radon_tiles, tile_blocks)))

    def angle_step(group):
        proj_angle, offset_row, amplitude_row, counts_row = group
        columns = (offset_row[:, None] + jnp.arange(PROBE, dtype=jnp.int32)[None, :]) % U
        patches = jnp.transpose(proj_angle[:, :, columns], (2, 0, 1, 3))
        slot_index = jnp.arange(POSITIONS, dtype=jnp.int32)
        live_mask = (slot_index % POS_DEV < counts_row[slot_index // POS_DEV]).astype(jnp.float32)
        patch_grads = exit_gradient(patches, probe_field, amplitude_row, live_mask)
        summed = jnp.zeros((2, SLICES, U), jnp.float32)
        return summed.at[:, :, columns].add(jnp.transpose(patch_grads, (1, 2, 0, 3)))
    grads = lax.map(angle_step, (projection, offsets, amplitudes, counts))
    proj_grad = jnp.transpose(grads, (1, 2, 0, 3))
    grad_rounded = rounded(grads)

    def backward(summed, group):
        grad_angle, tile_angle, ids_angle = group
        grad_blocks = grad_angle.reshape(2, SLICES, UB, BLOCK).astype(jnp.float32)
        contrib = jnp.einsum('csum,mx->csux', grad_blocks, tile_angle.astype(jnp.float32))
        contrib = contrib.reshape(2, SLICES, UB * J, BLOCK)
        return (summed.at[:, :, ids_angle.reshape(-1)].add(contrib), None)
    start_sum = jnp.zeros((2, SLICES, KB, BLOCK), jnp.float32)
    object_grad, unused_out = lax.scan(backward, start_sum, (grad_rounded, radon_tiles, tile_blocks))
    new_volume = volume.astype(jnp.float32) + step_size * object_grad.reshape(2, SLICES, KCOEF)
    return (new_volume, proj_grad)
```

```python
import functools
import math

import jax
import jax.numpy as jnp
from jax import lax
from jax.experimental import pallas as pl
from jax.experimental.pallas import tpu as pltpu
from jax.sharding import PartitionSpec as P

step_size = 0.1
f32 = jnp.float32
bf16 = jnp.bfloat16


def from_behind(block, axis, distance):
    devices = range(lax.axis_size(axis))
    route = [((i - distance) % len(devices), i) for i in devices]
    return lax.ppermute(block, axis, route)


def dft_tables(width):
    index = jnp.arange(width, dtype=jnp.int32)
    phase = index[:, None] * index[None, :] % width
    turn = 2.0 * math.pi / width * phase.astype(f32)
    cosine = (jnp.cos(turn) / math.sqrt(width)).astype(bf16)
    sine_neg = (-jnp.sin(turn) / math.sqrt(width)).astype(bf16)
    return (cosine, sine_neg)


def low_half(shape):
    return lax.broadcasted_iota(jnp.int32, shape, len(shape) - 1) < 64


def project_kernel(ids, vol, tiles, out, spread, *, feeds, pairs, angles):
    step = pl.program_id(0)
    owners, rows, width = vol.shape
    lo32 = low_half((rows, 128))

    @pl.when(step == 0)
    def _():
        per_owner = width // 128

        def expand(p, carry):
            at = pl.multiple_of(p * 128, 128)
            for o in range(owners):
                tile = vol[o, :, pl.ds(at, 128)].astype(f32)
                turned = pltpu.roll(tile, 64, 1)
                base = 2 * (o * per_owner + p)
                spread[base] = jnp.where(lo32, tile, turned).astype(bf16)
                spread[base + 1] = jnp.where(lo32, turned, tile).astype(bf16)
            return carry

        lax.fori_loop(0, per_owner, expand, 0, unroll=2)

    lo = low_half((rows, 128))
    for a in range(angles):
        at = (step * angles + a) * (2 * pairs * feeds)
        halves = []
        for parity in range(2):
            for bp in range(pairs):
                first = at + (2 * bp + parity) * feeds
                tile = [spread[ids[first + j]] for j in range(feeds)]
                halves.append(
                    jnp.concatenate(
                        [jnp.where(lo, tile[j], tile[j + 1]) for j in range(0, feeds, 2)], axis=1
                    )
                )
        picked = jnp.concatenate(halves, axis=0)
        twice = jnp.concatenate([tiles[a], tiles[a]], axis=0)
        both = lax.dot_general(
            picked, twice, (((1,), (1,)), ((), ())), preferred_element_type=f32
        )
        half = pairs * rows
        joined = jnp.where(low_half((half, 128)), both[:half], both[half:]).astype(bf16)
        for bp in range(pairs):
            out[0, a, :, bp * 128 : (bp + 1) * 128] = joined[bp * rows : (bp + 1) * rows]


def project(ids, vol, tiles, groups):
    owners, rows, width = vol.shape
    angle_count, block, span = tiles.shape
    feeds = span // block
    per_angle = ids.shape[0] // angle_count
    dets = per_angle // feeds
    angles = angle_count // groups
    blocks = owners * width // block
    return pl.pallas_call(
        functools.partial(project_kernel, feeds=feeds, pairs=dets // 2, angles=angles),
        name="project",
        out_shape=jax.ShapeDtypeStruct((groups, angles, rows, dets * block), bf16),
        grid_spec=pltpu.PrefetchScalarGridSpec(
            num_scalar_prefetch=1,
            grid=(groups,),
            in_specs=[
                pl.BlockSpec((owners, rows, width), lambda g, ids: (0, 0, 0)),
                pl.BlockSpec((angles, block, span), lambda g, ids: (g, 0, 0)),
            ],
            out_specs=pl.BlockSpec((1, angles, rows, dets * block), lambda g, ids: (g, 0, 0, 0)),
            scratch_shapes=[pltpu.VMEM((blocks, rows, 128), bf16)],
        ),
    )(ids, vol, tiles)


def exit_kernel(starts, counts, own, nextdoor, probe, amp, fwd, inv, grad, spill, ext, acc, *, slots):
    angle = pl.program_id(0)
    groups, _, rows, tile_width = own.shape
    side = probe.shape[1]
    n = groups * rows
    ext[:, :tile_width] = own[:, 0].reshape(n, tile_width)
    ext[:, tile_width:] = nextdoor[:, 0].reshape(n, side)
    acc[...] = jnp.zeros_like(acc)
    window = side + 128
    probe_re = probe[0].astype(f32)
    probe_im = probe[1].astype(f32)
    for slot in range(slots):
        start = starts[angle, slot]
        base = pl.multiple_of(start // 128 * 128, 128)
        shift = start - base
        source = lax.broadcasted_iota(jnp.int32, (window, side), 0)
        target = lax.broadcasted_iota(jnp.int32, (window, side), 1)
        pick = jnp.where(source - target == shift, 1.0, 0.0).astype(bf16)
        patch = jnp.dot(ext[:, pl.ds(base, window)], pick, preferred_element_type=f32)
        patch = patch.reshape(groups, 2, rows // 2, side)
        patch_re = patch[:, 0].reshape(side, side)
        patch_im = patch[:, 1].reshape(side, side)
        wave_re = (probe_re * patch_re - probe_im * patch_im).astype(bf16)
        wave_im = (probe_re * patch_im + probe_im * patch_re).astype(bf16)
        wave = jnp.concatenate([wave_re, wave_im], axis=0)
        half = jnp.dot(fwd[...], wave, preferred_element_type=f32).astype(bf16)
        half = jnp.concatenate([half[:side], half[side:]], axis=1)
        far = jnp.dot(half, inv[...], preferred_element_type=f32)
        far_re = far[:, :side]
        far_im = far[:, side:]
        power = far_re * far_re + far_im * far_im
        factor = amp[0, slot].astype(f32) * lax.rsqrt(jnp.maximum(power, 1.0)) - 1.0
        delta = jnp.concatenate(
            [(far_re * factor).astype(bf16), (far_im * factor).astype(bf16)], axis=0
        )
        back = jnp.dot(inv[...], delta, preferred_element_type=f32).astype(bf16)
        back = jnp.concatenate([back[:side], back[side:]], axis=1)
        near = jnp.dot(back, fwd[...], preferred_element_type=f32)
        near_re = near[:, :side]
        near_im = near[:, side:]
        live = jnp.where(slot < counts[angle, 0], 1.0, 0.0).astype(f32)
        grad_re = (probe_re * near_re + probe_im * near_im) * live
        grad_im = (probe_re * near_im - probe_im * near_re) * live
        both = jnp.concatenate(
            [
                grad_re.reshape(groups, 1, rows // 2, side),
                grad_im.reshape(groups, 1, rows // 2, side),
            ],
            axis=1,
        ).reshape(n, side)
        source = lax.broadcasted_iota(jnp.int32, (side, window), 1)
        target = lax.broadcasted_iota(jnp.int32, (side, window), 0)
        place = jnp.where(source - target == shift, 1.0, 0.0).astype(bf16)
        acc[:, pl.ds(base, window)] += jnp.dot(
            both.astype(bf16), place, preferred_element_type=f32
        )
    grad[:, 0] = acc[:, :tile_width].reshape(groups, rows, tile_width)
    spill[:, 0] = acc[:, tile_width:].astype(bf16).reshape(groups, rows, side)


def exit_gradient(starts, counts, own, nextdoor, probe, amp, fwd, inv):
    groups, angles, rows, tile_width = own.shape
    side = probe.shape[1]
    slots = starts.shape[1]
    n = groups * rows
    smem = pl.BlockSpec(memory_space=pltpu.SMEM)
    return pl.pallas_call(
        functools.partial(exit_kernel, slots=slots),
        name="exit_gradient",
        grid=(angles,),
        in_specs=[
            smem,
            smem,
            pl.BlockSpec((groups, 1, rows, tile_width), lambda a: (0, a, 0, 0)),
            pl.BlockSpec((groups, 1, rows, side), lambda a: (0, a, 0, 0)),
            pl.BlockSpec((2, side, side), lambda a: (0, 0, 0)),
            pl.BlockSpec((1, slots, side, side), lambda a: (a, 0, 0, 0)),
            pl.BlockSpec((2 * side, 2 * side), lambda a: (0, 0)),
            pl.BlockSpec((2 * side, 2 * side), lambda a: (0, 0)),
        ],
        out_specs=[
            pl.BlockSpec((groups, 1, rows, tile_width), lambda a: (0, a, 0, 0)),
            pl.BlockSpec((groups, 1, rows, side), lambda a: (0, a, 0, 0)),
        ],
        out_shape=[
            jax.ShapeDtypeStruct((groups, angles, rows, tile_width), f32),
            jax.ShapeDtypeStruct((groups, angles, rows, side), bf16),
        ],
        scratch_shapes=[
            pltpu.VMEM((n, tile_width + side), bf16),
            pltpu.VMEM((n, tile_width + side), f32),
        ],
    )(starts, counts, own, nextdoor, probe, amp, fwd, inv)


def back_kernel(ids, grad, tiles, out, *accs, feeds, pairs, angles):
    step = pl.program_id(0)
    owners, rows, width = out.shape
    blocks = accs[0].shape[0]

    @pl.when(step == 0)
    def _():
        def clear(i, carry):
            for acc in accs:
                acc[pl.ds(i * 8, 8)] = jnp.zeros((8, rows, 128), f32)
            return carry

        lax.fori_loop(0, blocks // 8, clear, 0)

    half = pairs * rows
    lo = low_half((half, 128))
    for a in range(angles):
        at = (step * angles + a) * (2 * pairs * feeds)
        flat = jnp.concatenate(
            [grad[0, a, :, bp * 128 : (bp + 1) * 128] for bp in range(pairs)], axis=0
        )
        zero = jnp.zeros_like(flat)
        halves = jnp.concatenate([jnp.where(lo, flat, zero), jnp.where(lo, zero, flat)], axis=0)
        twice = jnp.concatenate([tiles[a], tiles[a]], axis=0)
        contrib = jnp.dot(halves, twice, preferred_element_type=f32)
        for parity in range(2):
            for bp in range(pairs):
                first = at + (2 * bp + parity) * feeds
                top = (parity * pairs + bp) * rows
                where = [ids[first + j] for j in range(feeds)]
                old = [accs[j][where[j]] for j in range(feeds)]
                for j in range(feeds):
                    lane = j // 2 * 128
                    accs[j][where[j]] = old[j] + contrib[top : top + rows, lane : lane + 128]

    @pl.when(step == pl.num_programs(0) - 1)
    def _():
        lo = low_half((rows, 128))
        per_owner = width // 128

        def join(p, carry):
            at = pl.multiple_of(p * 128, 128)
            for o in range(owners):
                kb = 2 * (o * per_owner + p)
                even_lo = sum(accs[j][kb] for j in range(0, feeds, 2))
                even_hi = sum(accs[j][kb] for j in range(1, feeds, 2))
                odd_lo = sum(accs[j][kb + 1] for j in range(0, feeds, 2))
                odd_hi = sum(accs[j][kb + 1] for j in range(1, feeds, 2))
                out[o, :, pl.ds(at, 128)] = jnp.where(lo, even_lo, odd_hi) + pltpu.roll(
                    jnp.where(lo, odd_lo, even_hi), 64, 1
                )
            return carry

        lax.fori_loop(0, per_owner, join, 0, unroll=2)


def back_project(ids, grad, tiles, owners, coefs):
    groups, angles, rows, tile_width = grad.shape
    angle_count, block, span = tiles.shape
    feeds = span // block
    dets = tile_width // block
    blocks = coefs // block
    width = coefs // owners
    return pl.pallas_call(
        functools.partial(back_kernel, feeds=feeds, pairs=dets // 2, angles=angles),
        name="back_project",
        out_shape=jax.ShapeDtypeStruct((owners, rows, width), f32),
        grid_spec=pltpu.PrefetchScalarGridSpec(
            num_scalar_prefetch=1,
            grid=(groups,),
            in_specs=[
                pl.BlockSpec((1, angles, rows, tile_width), lambda g, ids: (g, 0, 0, 0)),
                pl.BlockSpec((angles, block, span), lambda g, ids: (g, 0, 0)),
            ],
            out_specs=pl.BlockSpec((owners, rows, width), lambda g, ids: (0, 0, 0)),
            scratch_shapes=[pltpu.VMEM((blocks, rows, 128), f32) for _ in range(feeds)],
        ),
    )(ids, grad, tiles)


def on_device(volume, radon_tiles, tile_blocks, probe_field, amplitudes, offsets, counts):
    n_pos = lax.axis_size("pos")
    n_ang = lax.axis_size("ang")
    pos_index = lax.axis_index("pos")
    parts, slab, width = volume.shape
    block = radon_tiles.shape[1]
    own_blocks = tile_blocks.shape[1] // n_pos
    tile_width = own_blocks * block
    side = probe_field.shape[1]
    angles = amplitudes.shape[0]
    rows = parts * slab

    whole = lax.all_gather(volume.reshape(rows, width), "pos", axis=0, tiled=False)
    ids = lax.dynamic_slice_in_dim(tile_blocks, pos_index * own_blocks, own_blocks, 1).reshape(-1)
    cosine, sine_neg = dft_tables(side)
    fwd = jnp.concatenate(
        [jnp.concatenate([cosine, -sine_neg], 1), jnp.concatenate([sine_neg, cosine], 1)], 0
    )
    inv = jnp.concatenate(
        [jnp.concatenate([cosine, sine_neg], 1), jnp.concatenate([-sine_neg, cosine], 1)], 0
    )
    starts = offsets - pos_index * tile_width

    sinogram = project(ids, whole, radon_tiles, n_ang)
    own = lax.all_to_all(sinogram, "ang", split_axis=0, concat_axis=0, tiled=True)
    nextdoor = from_behind(own[..., :side], "pos", -1)
    grad, spill = exit_gradient(
        starts, counts, own, nextdoor, probe_field, amplitudes, fwd, inv
    )
    spill = from_behind(spill, "pos", 1)
    grad = grad + jnp.pad(spill.astype(f32), ((0, 0), (0, 0), (0, 0), (0, tile_width - side)))
    back = lax.all_to_all(grad.astype(bf16), "ang", split_axis=0, concat_axis=0, tiled=True)
    partial = back_project(ids, back, radon_tiles, n_pos, n_pos * width)
    total = lax.psum_scatter(partial, "pos", scatter_dimension=0, tiled=False)
    new_volume = volume.astype(f32) + step_size * total.reshape(volume.shape)
    proj_grad = (
        grad.reshape(n_ang, angles, parts, slab, tile_width)
        .transpose(2, 0, 3, 1, 4)
        .reshape(parts, n_ang * slab, angles, tile_width)
    )
    return (new_volume, proj_grad)


def solution(mesh):
    in_specs = (
        P(None, "ang", "pos"),
        P(),
        P(),
        P(),
        P("ang", "pos", None, None),
        P("ang", "pos"),
        P("ang", "pos"),
    )
    out_specs = (P(None, "ang", "pos"), P(None, None, "ang", "pos"))
    return jax.shard_map(
        on_device, mesh=mesh, in_specs=in_specs, out_specs=out_specs, check_vma=False
    )
```

```python
import functools
import math

import jax
import jax.numpy as jnp
from jax import lax
from jax.experimental import pallas as pl
from jax.experimental.pallas import tpu as pltpu
from jax.sharding import PartitionSpec as P

step_size = 0.1
f32 = jnp.float32
bf16 = jnp.bfloat16
MESH = pl.DeviceIdType.MESH


def from_behind(block, axis, distance):
    devices = range(lax.axis_size(axis))
    route = [((i - distance) % len(devices), i) for i in devices]
    return lax.ppermute(block, axis, route)


def dft_tables(width):
    index = jnp.arange(width, dtype=jnp.int32)
    phase = index[:, None] * index[None, :] % width
    turn = 2.0 * math.pi / width * phase.astype(f32)
    cosine = (jnp.cos(turn) / math.sqrt(width)).astype(bf16)
    sine_neg = (-jnp.sin(turn) / math.sqrt(width)).astype(bf16)
    return (cosine, sine_neg)


def low_half(shape):
    return lax.broadcasted_iota(jnp.int32, shape, len(shape) - 1) < 64


def pos_peers():
    pos = lax.axis_index("pos")
    partner = pos + 1 - 2 * lax.rem(pos, 2)
    cross = lax.rem(pos + 2, 4)
    return pos, partner, cross


def ang_peer(step, forward):
    me = lax.axis_index("ang")
    offset = lax.rem(13 * (step + 1), 32)
    way = 1 - 2 * lax.rem(lax.axis_index("pos"), 2)
    way = way if forward else -way
    z = lax.rem(lax.div(me, 8) + way * lax.div(offset, 8) + 4, 4)
    y = lax.rem(lax.rem(lax.div(me, 2), 4) + way * lax.rem(lax.div(offset, 2), 4) + 4, 4)
    x = lax.rem(lax.rem(me, 2) + lax.rem(offset, 2), 2)
    return z * 8 + y * 2 + x


def remote(src, dst, send_sem, recv_sem, device):
    return pltpu.make_async_remote_copy(
        src_ref=src,
        dst_ref=dst,
        send_sem=send_sem,
        recv_sem=recv_sem,
        device_id=device,
        device_id_type=MESH,
    )


def project_kernel(
    ids, vol, tiles_hbm, out, gathered, tiles, spread, ready, tile_sem, own_sem, pos_send, pos_recv,
    ang_send, ang_recv, *, feeds, pairs, angles, groups
):
    rows, width = vol.shape
    me = lax.axis_index("ang")
    pos, partner, cross = pos_peers()
    far = lax.rem(partner + 2, 4)
    load = pltpu.make_async_copy(tiles_hbm, tiles, tile_sem)
    load.start()

    barrier = pltpu.get_barrier_semaphore()
    pl.semaphore_signal(barrier, inc=1, device_id={"pos": partner}, device_id_type=MESH)
    pl.semaphore_signal(barrier, inc=1, device_id={"pos": cross}, device_id_type=MESH)

    def greet(step, carry):
        pl.semaphore_signal(
            barrier, inc=1, device_id={"ang": ang_peer(step, True)}, device_id_type=MESH
        )
        return carry

    lax.fori_loop(0, groups - 1, greet, 0)
    pl.semaphore_wait(barrier, groups + 1)

    to_cross = remote(vol, gathered.at[1], pos_send.at[1], pos_recv.at[1], {"pos": cross})
    to_partner = remote(vol, gathered.at[0], pos_send.at[0], pos_recv.at[0], {"pos": partner})
    onward = remote(
        gathered.at[1], gathered.at[2], pos_send.at[2], pos_recv.at[2], {"pos": partner}
    )
    to_cross.start()
    to_partner.start()

    lo32 = low_half((rows, 128))
    per_owner = width // 128

    def expand(source, owner):
        def body(p, carry):
            at = pl.multiple_of(p * 128, 128)
            tile = source[:, pl.ds(at, 128)].astype(f32)
            turned = pltpu.roll(tile, 64, 1)
            base = 2 * (owner * per_owner + p)
            spread[base] = jnp.where(lo32, tile, turned).astype(bf16)
            spread[base + 1] = jnp.where(lo32, turned, tile).astype(bf16)
            return carry

        lax.fori_loop(0, per_owner, body, 0, unroll=4)

    expand(vol, pos)
    to_partner.wait_recv()
    expand(gathered.at[0], partner)
    to_cross.wait_recv()
    onward.start()
    expand(gathered.at[1], cross)
    load.wait()
    onward.wait_recv()
    expand(gathered.at[2], far)

    def outgoing(step):
        group = ang_peer(step, True)
        return remote(
            ready.at[group], out.at[me], ang_send.at[step], ang_recv.at[step], {"ang": group}
        )

    def incoming(step):
        group = ang_peer(step, False)
        return remote(
            ready.at[group], out.at[group], ang_send.at[step], ang_recv.at[step], {"ang": group}
        )

    lo = low_half((rows, 128))
    half = pairs * rows
    lo_half = low_half((half, 128))

    def group_step(step, carry):
        @pl.when(step > 0)
        def _():
            outgoing(step - 1).start()

        group = ang_peer(step, True)
        for a in range(angles):
            at = (group * angles + a) * (2 * pairs * feeds)
            halves = []
            for parity in range(2):
                for bp in range(pairs):
                    first = at + (2 * bp + parity) * feeds
                    tile = [spread[ids[first + j]] for j in range(feeds)]
                    halves.append(
                        jnp.concatenate(
                            [jnp.where(lo, tile[j], tile[j + 1]) for j in range(0, feeds, 2)],
                            axis=1,
                        )
                    )
            picked = jnp.concatenate(halves, axis=0)
            radon = tiles[group * angles + a]
            twice = jnp.concatenate([radon, radon], axis=0)
            both = lax.dot_general(
                picked, twice, (((1,), (1,)), ((), ())), preferred_element_type=f32
            )
            joined = jnp.where(lo_half, both[:half], both[half:]).astype(bf16)
            for bp in range(pairs):
                ready[group, a, :, bp * 128 : (bp + 1) * 128] = joined[bp * rows : (bp + 1) * rows]
        return carry

    lax.fori_loop(0, groups, group_step, 0)
    to_cross.wait_send()
    to_partner.wait_send()
    onward.wait_send()
    mine = pltpu.make_async_copy(ready.at[me], out.at[me], own_sem)
    mine.start()

    def finish(step, carry):
        outgoing(step).wait_send()
        incoming(step).wait_recv()
        return carry

    lax.fori_loop(0, groups - 1, finish, 0)
    mine.wait()


def project(ids, vol, tiles, groups, owners):
    rows, width = vol.shape
    angle_count, block, span = tiles.shape
    feeds = span // block
    per_angle = ids.shape[0] // angle_count
    dets = per_angle // feeds
    angles = angle_count // groups
    blocks = owners * width // block
    dma = pltpu.SemaphoreType.DMA
    return pl.pallas_call(
        functools.partial(
            project_kernel, feeds=feeds, pairs=dets // 2, angles=angles, groups=groups
        ),
        name="project",
        out_shape=jax.ShapeDtypeStruct((groups, angles, rows, dets * block), bf16),
        in_specs=[
            pl.BlockSpec(memory_space=pltpu.SMEM),
            pl.BlockSpec(memory_space=pltpu.VMEM),
            pl.BlockSpec(memory_space=pl.ANY),
        ],
        out_specs=pl.BlockSpec(memory_space=pl.ANY),
        scratch_shapes=[
            pltpu.VMEM((owners - 1, rows, width), bf16),
            pltpu.VMEM(tiles.shape, bf16),
            pltpu.VMEM((blocks, rows, 128), bf16),
            pltpu.VMEM((groups, angles, rows, dets * block), bf16),
            dma,
            dma,
            dma((3,)),
            dma((3,)),
            dma((groups - 1,)),
            dma((groups - 1,)),
        ],
        compiler_params=pltpu.CompilerParams(collective_id=0, has_side_effects=True),
    )(ids, vol, tiles)


def exit_kernel(starts, counts, own, nextdoor, probe, amp, fwd, inv, grad, spill, ext, acc, *, slots):
    angle = pl.program_id(0)
    groups, _, rows, tile_width = own.shape
    side = probe.shape[1]
    n = groups * rows
    ext[:, :tile_width] = own[:, 0].reshape(n, tile_width)
    ext[:, tile_width:] = nextdoor[:, 0].reshape(n, side)
    acc[...] = jnp.zeros_like(acc)
    window = side + 128
    probe_re = probe[0].astype(f32)
    probe_im = probe[1].astype(f32)
    for slot in range(slots):
        start = starts[angle, slot]
        base = pl.multiple_of(start // 128 * 128, 128)
        shift = start - base
        source = lax.broadcasted_iota(jnp.int32, (window, side), 0)
        target = lax.broadcasted_iota(jnp.int32, (window, side), 1)
        pick = jnp.where(source - target == shift, 1.0, 0.0).astype(bf16)
        patch = jnp.dot(ext[:, pl.ds(base, window)], pick, preferred_element_type=f32)
        patch = patch.reshape(groups, 2, rows // 2, side)
        patch_re = patch[:, 0].reshape(side, side)
        patch_im = patch[:, 1].reshape(side, side)
        wave_re = (probe_re * patch_re - probe_im * patch_im).astype(bf16)
        wave_im = (probe_re * patch_im + probe_im * patch_re).astype(bf16)
        wave = jnp.concatenate([wave_re, wave_im], axis=0)
        half = jnp.dot(fwd[...], wave, preferred_element_type=f32).astype(bf16)
        half = jnp.concatenate([half[:side], half[side:]], axis=1)
        far = jnp.dot(half, inv[...], preferred_element_type=f32)
        far_re = far[:, :side]
        far_im = far[:, side:]
        power = far_re * far_re + far_im * far_im
        factor = amp[0, slot].astype(f32) * lax.rsqrt(jnp.maximum(power, 1.0)) - 1.0
        delta = jnp.concatenate(
            [(far_re * factor).astype(bf16), (far_im * factor).astype(bf16)], axis=0
        )
        back = jnp.dot(inv[...], delta, preferred_element_type=f32).astype(bf16)
        back = jnp.concatenate([back[:side], back[side:]], axis=1)
        near = jnp.dot(back, fwd[...], preferred_element_type=f32)
        near_re = near[:, :side]
        near_im = near[:, side:]
        live = jnp.where(slot < counts[angle, 0], 1.0, 0.0).astype(f32)
        grad_re = (probe_re * near_re + probe_im * near_im) * live
        grad_im = (probe_re * near_im - probe_im * near_re) * live
        both = jnp.concatenate(
            [
                grad_re.reshape(groups, 1, rows // 2, side),
                grad_im.reshape(groups, 1, rows // 2, side),
            ],
            axis=1,
        ).reshape(n, side)
        source = lax.broadcasted_iota(jnp.int32, (side, window), 1)
        target = lax.broadcasted_iota(jnp.int32, (side, window), 0)
        place = jnp.where(source - target == shift, 1.0, 0.0).astype(bf16)
        acc[:, pl.ds(base, window)] += jnp.dot(
            both.astype(bf16), place, preferred_element_type=f32
        )
    grad[:, 0] = acc[:, :tile_width].reshape(groups, rows, tile_width)
    spill[:, 0] = acc[:, tile_width:].astype(bf16).reshape(groups, rows, side)


def exit_gradient(starts, counts, own, nextdoor, probe, amp, fwd, inv):
    groups, angles, rows, tile_width = own.shape
    side = probe.shape[1]
    slots = starts.shape[1]
    n = groups * rows
    smem = pl.BlockSpec(memory_space=pltpu.SMEM)
    return pl.pallas_call(
        functools.partial(exit_kernel, slots=slots),
        name="exit_gradient",
        grid=(angles,),
        in_specs=[
            smem,
            smem,
            pl.BlockSpec((groups, 1, rows, tile_width), lambda a: (0, a, 0, 0)),
            pl.BlockSpec((groups, 1, rows, side), lambda a: (0, a, 0, 0)),
            pl.BlockSpec((2, side, side), lambda a: (0, 0, 0)),
            pl.BlockSpec((1, slots, side, side), lambda a: (a, 0, 0, 0)),
            pl.BlockSpec((2 * side, 2 * side), lambda a: (0, 0)),
            pl.BlockSpec((2 * side, 2 * side), lambda a: (0, 0)),
        ],
        out_specs=[
            pl.BlockSpec((groups, 1, rows, tile_width), lambda a: (0, a, 0, 0)),
            pl.BlockSpec((groups, 1, rows, side), lambda a: (0, a, 0, 0)),
        ],
        out_shape=[
            jax.ShapeDtypeStruct((groups, angles, rows, tile_width), f32),
            jax.ShapeDtypeStruct((groups, angles, rows, side), bf16),
        ],
        scratch_shapes=[
            pltpu.VMEM((n, tile_width + side), bf16),
            pltpu.VMEM((n, tile_width + side), f32),
        ],
    )(starts, counts, own, nextdoor, probe, amp, fwd, inv)


def back_kernel(ids, grad, tiles, out, *accs, feeds, pairs, angles):
    step = pl.program_id(0)
    owners, rows, width = out.shape
    blocks = accs[0].shape[0]

    @pl.when(step == 0)
    def _():
        def clear(i, carry):
            for acc in accs:
                acc[pl.ds(i * 8, 8)] = jnp.zeros((8, rows, 128), f32)
            return carry

        lax.fori_loop(0, blocks // 8, clear, 0)

    half = pairs * rows
    lo = low_half((half, 128))
    for a in range(angles):
        at = (step * angles + a) * (2 * pairs * feeds)
        flat = jnp.concatenate(
            [grad[0, a, :, bp * 128 : (bp + 1) * 128] for bp in range(pairs)], axis=0
        )
        zero = jnp.zeros_like(flat)
        halves = jnp.concatenate([jnp.where(lo, flat, zero), jnp.where(lo, zero, flat)], axis=0)
        twice = jnp.concatenate([tiles[a], tiles[a]], axis=0)
        contrib = jnp.dot(halves, twice, preferred_element_type=f32)
        for parity in range(2):
            for bp in range(pairs):
                first = at + (2 * bp + parity) * feeds
                top = (parity * pairs + bp) * rows
                where = [ids[first + j] for j in range(feeds)]
                old = [accs[j][where[j]] for j in range(feeds)]
                for j in range(feeds):
                    lane = j // 2 * 128
                    accs[j][where[j]] = old[j] + contrib[top : top + rows, lane : lane + 128]

    @pl.when(step == pl.num_programs(0) - 1)
    def _():
        lo = low_half((rows, 128))
        per_owner = width // 128

        def join(p, carry):
            at = pl.multiple_of(p * 128, 128)
            for o in range(owners):
                kb = 2 * (o * per_owner + p)
                even_lo = sum(accs[j][kb] for j in range(0, feeds, 2))
                even_hi = sum(accs[j][kb] for j in range(1, feeds, 2))
                odd_lo = sum(accs[j][kb + 1] for j in range(0, feeds, 2))
                odd_hi = sum(accs[j][kb + 1] for j in range(1, feeds, 2))
                joined = jnp.where(lo, even_lo, odd_hi) + pltpu.roll(
                    jnp.where(lo, odd_lo, even_hi), 64, 1
                )
                out[o, :, pl.ds(at, 128)] = joined.astype(bf16)
            return carry

        lax.fori_loop(0, per_owner, join, 0, unroll=2)


def back_project(ids, grad, tiles, owners, coefs):
    groups, angles, rows, tile_width = grad.shape
    angle_count, block, span = tiles.shape
    feeds = span // block
    dets = tile_width // block
    blocks = coefs // block
    width = coefs // owners
    return pl.pallas_call(
        functools.partial(back_kernel, feeds=feeds, pairs=dets // 2, angles=angles),
        name="back_project",
        out_shape=jax.ShapeDtypeStruct((owners, rows, width), bf16),
        grid_spec=pltpu.PrefetchScalarGridSpec(
            num_scalar_prefetch=1,
            grid=(groups,),
            in_specs=[
                pl.BlockSpec((1, angles, rows, tile_width), lambda g, ids: (g, 0, 0, 0)),
                pl.BlockSpec((angles, block, span), lambda g, ids: (g, 0, 0)),
            ],
            out_specs=pl.BlockSpec((owners, rows, width), lambda g, ids: (0, 0, 0)),
            scratch_shapes=[pltpu.VMEM((blocks, rows, 128), f32) for _ in range(feeds)],
        ),
    )(ids, grad, tiles)


def reduce_kernel(share, vol, out, near, mixed, far, send, recv):
    rows, width = vol.shape
    pos, partner, cross = pos_peers()
    beyond = lax.rem(partner + 2, 4)
    barrier = pltpu.get_barrier_semaphore()
    pl.semaphore_signal(barrier, inc=1, device_id={"pos": partner}, device_id_type=MESH)
    pl.semaphore_signal(barrier, inc=1, device_id={"pos": cross}, device_id_type=MESH)
    pl.semaphore_wait(barrier, 2)

    pieces = 4
    piece = width // pieces
    chunk = 512

    def columns(k):
        return pl.ds(k * piece, piece)

    def side(k):
        return remote(
            share.at[beyond, :, columns(k)], near.at[0, :, columns(k)], send.at[k], recv.at[k],
            {"pos": partner},
        )

    def over(k):
        return remote(
            mixed.at[:, columns(k)], far.at[:, columns(k)], send.at[pieces + k],
            recv.at[pieces + k], {"pos": cross},
        )

    home = remote(
        share.at[partner], near.at[1], send.at[2 * pieces], recv.at[2 * pieces], {"pos": partner}
    )
    for k in range(pieces):
        side(k).start()
    home.start()

    def mix(k):
        def body(i, carry):
            at = pl.ds(pl.multiple_of(k * piece + i * chunk, chunk), chunk)
            both = share[cross, :, at].astype(f32) + near[0, :, at].astype(f32)
            mixed[:, at] = both.astype(bf16)
            return carry

        lax.fori_loop(0, piece // chunk, body, 0)

    def total(k):
        def body(i, carry):
            at = pl.ds(pl.multiple_of(k * piece + i * chunk, chunk), chunk)
            both = share[pos, :, at].astype(f32) + near[1, :, at].astype(f32)
            out[:, at] = vol[:, at].astype(f32) + step_size * (both + far[:, at].astype(f32))
            return carry

        lax.fori_loop(0, piece // chunk, body, 0)

    for k in range(pieces):
        side(k).wait_recv()
        mix(k)
        if k > 0:
            over(k - 1).start()
    home.wait_recv()
    over(pieces - 1).start()
    for k in range(pieces):
        over(k).wait_recv()
        total(k)
    for k in range(pieces):
        side(k).wait_send()
        over(k).wait_send()
    home.wait_send()


def reduce_step(share, vol):
    rows, width = vol.shape
    vmem = pl.BlockSpec(memory_space=pltpu.VMEM)
    dma = pltpu.SemaphoreType.DMA
    return pl.pallas_call(
        reduce_kernel,
        name="reduce_step",
        out_shape=jax.ShapeDtypeStruct((rows, width), f32),
        in_specs=[vmem, vmem],
        out_specs=vmem,
        scratch_shapes=[
            pltpu.VMEM((2, rows, width), bf16),
            pltpu.VMEM((rows, width), bf16),
            pltpu.VMEM((rows, width), bf16),
            dma((9,)),
            dma((9,)),
        ],
        compiler_params=pltpu.CompilerParams(collective_id=1, has_side_effects=True),
    )(share, vol)


def on_device(volume, radon_tiles, tile_blocks, probe_field, amplitudes, offsets, counts):
    n_pos = lax.axis_size("pos")
    n_ang = lax.axis_size("ang")
    pos_index = lax.axis_index("pos")
    parts, slab, width = volume.shape
    block = radon_tiles.shape[1]
    own_blocks = tile_blocks.shape[1] // n_pos
    tile_width = own_blocks * block
    side = probe_field.shape[1]
    angles = amplitudes.shape[0]
    rows = parts * slab

    held = volume.reshape(rows, width)
    ids = lax.dynamic_slice_in_dim(tile_blocks, pos_index * own_blocks, own_blocks, 1).reshape(-1)
    cosine, sine_neg = dft_tables(side)
    fwd = jnp.concatenate(
        [jnp.concatenate([cosine, -sine_neg], 1), jnp.concatenate([sine_neg, cosine], 1)], 0
    )
    inv = jnp.concatenate(
        [jnp.concatenate([cosine, sine_neg], 1), jnp.concatenate([-sine_neg, cosine], 1)], 0
    )
    starts = offsets - pos_index * tile_width

    own = project(ids, held, radon_tiles, n_ang, n_pos)
    nextdoor = from_behind(own[..., :side], "pos", -1)
    grad, spill = exit_gradient(
        starts, counts, own, nextdoor, probe_field, amplitudes, fwd, inv
    )
    spill = from_behind(spill, "pos", 1)
    grad = grad + jnp.pad(spill.astype(f32), ((0, 0), (0, 0), (0, 0), (0, tile_width - side)))
    back = lax.all_to_all(grad.astype(bf16), "ang", split_axis=0, concat_axis=0, tiled=True)
    share = back_project(ids, back, radon_tiles, n_pos, n_pos * width)
    new_volume = reduce_step(share, held).reshape(volume.shape)
    proj_grad = (
        grad.reshape(n_ang, angles, parts, slab, tile_width)
        .transpose(2, 0, 3, 1, 4)
        .reshape(parts, n_ang * slab, angles, tile_width)
    )
    return (new_volume, proj_grad)


def solution(mesh):
    in_specs = (
        P(None, "ang", "pos"),
        P(),
        P(),
        P(),
        P("ang", "pos", None, None),
        P("ang", "pos"),
        P("ang", "pos"),
    )
    out_specs = (P(None, "ang", "pos"), P(None, None, "ang", "pos"))
    return jax.shard_map(
        on_device, mesh=mesh, in_specs=in_specs, out_specs=out_specs, check_vma=False
    )
```

```python
import functools
import math

import jax
import jax.numpy as jnp
from jax import lax
from jax.experimental import pallas as pl
from jax.experimental.pallas import tpu as pltpu
from jax.sharding import PartitionSpec as P

step_size = 0.1
f32 = jnp.float32
bf16 = jnp.bfloat16
MESH = pl.DeviceIdType.MESH


def dft_tables(width):
    index = jnp.arange(width, dtype=jnp.int32)
    phase = index[:, None] * index[None, :] % width
    turn = 2.0 * math.pi / width * phase.astype(f32)
    cosine = (jnp.cos(turn) / math.sqrt(width)).astype(bf16)
    sine_neg = (-jnp.sin(turn) / math.sqrt(width)).astype(bf16)
    return (cosine, sine_neg)


def low_half(shape):
    return lax.broadcasted_iota(jnp.int32, shape, len(shape) - 1) < 64


def pos_peers():
    pos = lax.axis_index("pos")
    partner = pos + 1 - 2 * lax.rem(pos, 2)
    cross = lax.rem(pos + 2, 4)
    return pos, partner, cross


def ang_peer(step, forward):
    me = lax.axis_index("ang")
    offset = lax.rem(13 * (step + 1), 32)
    way = 1 - 2 * lax.rem(lax.axis_index("pos"), 2)
    way = way if forward else -way
    z = lax.rem(lax.div(me, 8) + way * lax.div(offset, 8) + 4, 4)
    y = lax.rem(lax.rem(lax.div(me, 2), 4) + way * lax.rem(lax.div(offset, 2), 4) + 4, 4)
    x = lax.rem(lax.rem(me, 2) + lax.rem(offset, 2), 2)
    return z * 8 + y * 2 + x


def remote(src, dst, send_sem, recv_sem, device):
    return pltpu.make_async_remote_copy(
        src_ref=src,
        dst_ref=dst,
        send_sem=send_sem,
        recv_sem=recv_sem,
        device_id=device,
        device_id_type=MESH,
    )


def project_kernel(
    ids, vol, tiles_hbm, out, gathered, tiles, spread, ready, tile_sem, own_sem, pos_send, pos_recv,
    ang_send, ang_recv, *, feeds, pairs, angles, groups
):
    rows, width = vol.shape
    me = lax.axis_index("ang")
    pos, partner, cross = pos_peers()
    far = lax.rem(partner + 2, 4)
    load = pltpu.make_async_copy(tiles_hbm, tiles, tile_sem)
    load.start()

    barrier = pltpu.get_barrier_semaphore()
    pl.semaphore_signal(barrier, inc=1, device_id={"pos": partner}, device_id_type=MESH)
    pl.semaphore_signal(barrier, inc=1, device_id={"pos": cross}, device_id_type=MESH)

    def greet(step, carry):
        pl.semaphore_signal(
            barrier, inc=1, device_id={"ang": ang_peer(step, True)}, device_id_type=MESH
        )
        return carry

    lax.fori_loop(0, groups - 1, greet, 0)
    pl.semaphore_wait(barrier, groups + 1)

    to_cross = remote(vol, gathered.at[1], pos_send.at[1], pos_recv.at[1], {"pos": cross})
    to_partner = remote(vol, gathered.at[0], pos_send.at[0], pos_recv.at[0], {"pos": partner})
    onward = remote(
        gathered.at[1], gathered.at[2], pos_send.at[2], pos_recv.at[2], {"pos": partner}
    )
    to_cross.start()
    to_partner.start()

    lo32 = low_half((rows, 128))
    per_owner = width // 128

    def expand(source, owner):
        def body(p, carry):
            at = pl.multiple_of(p * 128, 128)
            tile = source[:, pl.ds(at, 128)].astype(f32)
            turned = pltpu.roll(tile, 64, 1)
            base = 2 * (owner * per_owner + p)
            spread[base] = jnp.where(lo32, tile, turned).astype(bf16)
            spread[base + 1] = jnp.where(lo32, turned, tile).astype(bf16)
            return carry

        lax.fori_loop(0, per_owner, body, 0, unroll=4)

    expand(vol, pos)
    to_partner.wait_recv()
    expand(gathered.at[0], partner)
    to_cross.wait_recv()
    onward.start()
    expand(gathered.at[1], cross)
    load.wait()
    onward.wait_recv()
    expand(gathered.at[2], far)

    def outgoing(step):
        group = ang_peer(step, True)
        return remote(
            ready.at[group], out.at[me], ang_send.at[step], ang_recv.at[step], {"ang": group}
        )

    def incoming(step):
        group = ang_peer(step, False)
        return remote(
            ready.at[group], out.at[group], ang_send.at[step], ang_recv.at[step], {"ang": group}
        )

    lo = low_half((rows, 128))
    half = pairs * rows
    lo_half = low_half((half, 128))

    def group_step(step, carry):
        @pl.when(step > 0)
        def _():
            outgoing(step - 1).start()

        group = ang_peer(step, True)
        for a in range(angles):
            at = (group * angles + a) * (2 * pairs * feeds)
            halves = []
            for parity in range(2):
                for bp in range(pairs):
                    first = at + (2 * bp + parity) * feeds
                    tile = [spread[ids[first + j]] for j in range(feeds)]
                    halves.append(
                        jnp.concatenate(
                            [jnp.where(lo, tile[j], tile[j + 1]) for j in range(0, feeds, 2)],
                            axis=1,
                        )
                    )
            picked = jnp.concatenate(halves, axis=0)
            radon = tiles[group * angles + a]
            twice = jnp.concatenate([radon, radon], axis=0)
            both = lax.dot_general(
                picked, twice, (((1,), (1,)), ((), ())), preferred_element_type=f32
            )
            joined = jnp.where(lo_half, both[:half], both[half:]).astype(bf16)
            for bp in range(pairs):
                ready[group, a, :, bp * 128 : (bp + 1) * 128] = joined[bp * rows : (bp + 1) * rows]
        return carry

    lax.fori_loop(0, groups, group_step, 0)
    to_cross.wait_send()
    to_partner.wait_send()
    onward.wait_send()
    mine = pltpu.make_async_copy(ready.at[me], out.at[me], own_sem)
    mine.start()

    def finish(step, carry):
        outgoing(step).wait_send()
        incoming(step).wait_recv()
        return carry

    lax.fori_loop(0, groups - 1, finish, 0)
    mine.wait()


def project(ids, vol, tiles, groups, owners):
    rows, width = vol.shape
    angle_count, block, span = tiles.shape
    feeds = span // block
    per_angle = ids.shape[0] // angle_count
    dets = per_angle // feeds
    angles = angle_count // groups
    blocks = owners * width // block
    dma = pltpu.SemaphoreType.DMA
    return pl.pallas_call(
        functools.partial(
            project_kernel, feeds=feeds, pairs=dets // 2, angles=angles, groups=groups
        ),
        name="project",
        out_shape=jax.ShapeDtypeStruct((groups, angles, rows, dets * block), bf16),
        in_specs=[
            pl.BlockSpec(memory_space=pltpu.SMEM),
            pl.BlockSpec(memory_space=pltpu.VMEM),
            pl.BlockSpec(memory_space=pl.ANY),
        ],
        out_specs=pl.BlockSpec(memory_space=pl.ANY),
        scratch_shapes=[
            pltpu.VMEM((owners - 1, rows, width), bf16),
            pltpu.VMEM(tiles.shape, bf16),
            pltpu.VMEM((blocks, rows, 128), bf16),
            pltpu.VMEM((groups, angles, rows, dets * block), bf16),
            dma,
            dma,
            dma((3,)),
            dma((3,)),
            dma((groups - 1,)),
            dma((groups - 1,)),
        ],
        compiler_params=pltpu.CompilerParams(collective_id=0, has_side_effects=True),
    )(ids, vol, tiles)


def exit_kernel(
    starts, counts, own, probe, amp, fwd, inv, grad, back, landed, strip, summed, rounded, patches,
    spill_out, spill_in, load_sem, store_sem, own_sem, pos_send, pos_recv, ang_send, ang_recv,
    *, slots, groups, angles
):
    rows, tile_width = own.shape[2:]
    side = probe.shape[1]
    n = groups * rows
    me = lax.axis_index("ang")
    pos = lax.axis_index("pos")
    after = lax.rem(pos + 1, 4)
    before = lax.rem(pos + 3, 4)

    def load(a):
        return pltpu.make_async_copy(
            own.at[:, a], landed.at[a, :, :, :tile_width], load_sem.at[a]
        )

    def halo(a):
        return remote(
            own.at[:, a, :, :side], landed.at[a, :, :, tile_width:], pos_send.at[0, a],
            pos_recv.at[0, a], {"pos": before},
        )

    def spill(a):
        return remote(
            spill_out.at[a], spill_in.at[a], pos_send.at[1, a], pos_recv.at[1, a], {"pos": after}
        )

    def outgoing(a, step):
        group = ang_peer(step, True)
        return remote(
            rounded.at[a, group], back.at[me, a], ang_send.at[a, step], ang_recv.at[a, step],
            {"ang": group},
        )

    def incoming(a, step):
        group = ang_peer(step, False)
        return remote(
            rounded.at[a, group], back.at[group, a], ang_send.at[a, step], ang_recv.at[a, step],
            {"ang": group},
        )

    def keep(a):
        return pltpu.make_async_copy(rounded.at[a, me], back.at[me, a], own_sem.at[a])

    def store(a, c):
        half = rows // 2
        return pltpu.make_async_copy(
            summed.at[a, :, c * half : (c + 1) * half], grad.at[c, :, :, a, :], store_sem.at[a, c]
        )

    for a in range(angles):
        load(a).start()
    barrier = pltpu.get_barrier_semaphore()
    pl.semaphore_signal(barrier, inc=1, device_id={"pos": before}, device_id_type=MESH)
    pl.semaphore_signal(barrier, inc=1, device_id={"pos": after}, device_id_type=MESH)

    def greet(step, carry):
        pl.semaphore_signal(
            barrier, inc=1, device_id={"ang": ang_peer(step, True)}, device_id_type=MESH
        )
        return carry

    lax.fori_loop(0, groups - 1, greet, 0)
    pl.semaphore_wait(barrier, groups + 1)
    for a in range(angles):
        halo(a).start()

    window = side + 128
    probe_re = probe[0].astype(f32)
    probe_im = probe[1].astype(f32)

    def compute(a):
        load(a).wait()
        halo(a).wait_recv()
        for lane in range((tile_width + side) // 128):
            part = landed[a, :, :, lane * 128 : (lane + 1) * 128]
            strip[lane] = part.reshape(n, 128)
        for slot in range(slots):
            start = starts[a, slot]
            block = lax.div(start, 128)
            shift = start - block * 128
            source = lax.broadcasted_iota(jnp.int32, (window, side), 0)
            target = lax.broadcasted_iota(jnp.int32, (window, side), 1)
            pick = jnp.where(source - target == shift, 1.0, 0.0).astype(bf16)
            view = jnp.concatenate([strip[block + i] for i in range(window // 128)], axis=1)
            patch = jnp.dot(view, pick, preferred_element_type=f32)
            patch = patch.reshape(groups, 2, rows // 2, side)
            patch_re = patch[:, 0].reshape(side, side)
            patch_im = patch[:, 1].reshape(side, side)
            wave_re = (probe_re * patch_re - probe_im * patch_im).astype(bf16)
            wave_im = (probe_re * patch_im + probe_im * patch_re).astype(bf16)
            wave = jnp.concatenate([wave_re, wave_im], axis=0)
            half = jnp.dot(fwd[...], wave, preferred_element_type=f32).astype(bf16)
            half = jnp.concatenate([half[:side], half[side:]], axis=1)
            far = jnp.dot(half, inv[...], preferred_element_type=f32)
            far_re = far[:, :side]
            far_im = far[:, side:]
            power = far_re * far_re + far_im * far_im
            factor = amp[a, slot].astype(f32) * lax.rsqrt(jnp.maximum(power, 1.0)) - 1.0
            delta = jnp.concatenate(
                [(far_re * factor).astype(bf16), (far_im * factor).astype(bf16)], axis=0
            )
            turned = jnp.dot(inv[...], delta, preferred_element_type=f32).astype(bf16)
            turned = jnp.concatenate([turned[:side], turned[side:]], axis=1)
            near = jnp.dot(turned, fwd[...], preferred_element_type=f32)
            near_re = near[:, :side]
            near_im = near[:, side:]
            live = jnp.minimum(jnp.maximum(counts[a, 0] - slot, 0), 1).astype(f32)
            grad_re = (probe_re * near_re + probe_im * near_im) * live
            grad_im = (probe_re * near_im - probe_im * near_re) * live
            both = jnp.concatenate(
                [
                    grad_re.reshape(groups, 1, rows // 2, side),
                    grad_im.reshape(groups, 1, rows // 2, side),
                ],
                axis=1,
            ).reshape(n, side)
            patches[:, slot * side : (slot + 1) * side] = both.astype(bf16)
        whole = tile_width + side
        source = lax.broadcasted_iota(jnp.int32, (side, whole), 1)
        target = lax.broadcasted_iota(jnp.int32, (side, whole), 0)
        place = jnp.concatenate(
            [
                jnp.where(source - target == starts[a, slot], 1.0, 0.0).astype(bf16)
                for slot in range(slots)
            ],
            axis=0,
        )
        over = jnp.dot(patches[...], place[:, tile_width:], preferred_element_type=f32)
        spill_out[a] = over.astype(bf16).reshape(groups, rows, side)
        inside = jnp.dot(patches[...], place[:, :tile_width], preferred_element_type=f32)
        summed[a] = inside.reshape(groups, rows, tile_width)
        spill(a).start()

    def send(a):
        spill(a).wait_recv()

        def body(g, carry):
            left = summed[a, g, :, :side] + spill_in[a, g].astype(f32)
            summed[a, g, :, :side] = left
            rounded[a, g, :, :side] = left.astype(bf16)
            rounded[a, g, :, side:] = summed[a, g, :, side:].astype(bf16)
            return carry

        lax.fori_loop(0, groups, body, 0, unroll=2)
        for c in range(2):
            store(a, c).start()

        def depart(step, carry):
            outgoing(a, step).start()
            return carry

        lax.fori_loop(0, groups - 1, depart, 0)
        keep(a).start()

    def angle_step(a, carry):
        compute(a)

        @pl.when(a > 0)
        def _():
            send(a - 1)

        return carry

    lax.fori_loop(0, angles, angle_step, 0)
    send(angles - 1)
    for a in range(angles):
        halo(a).wait_send()
        spill(a).wait_send()
        keep(a).wait()
        for c in range(2):
            store(a, c).wait()

    def finish(step, carry):
        for a in range(angles):
            outgoing(a, step).wait_send()
            incoming(a, step).wait_recv()
        return carry

    lax.fori_loop(0, groups - 1, finish, 0)


def exit_gradient(starts, counts, own, probe, amp, fwd, inv):
    groups, angles, rows, tile_width = own.shape
    side = probe.shape[1]
    slots = starts.shape[1]
    n = groups * rows
    smem = pl.BlockSpec(memory_space=pltpu.SMEM)
    vmem = pl.BlockSpec(memory_space=pltpu.VMEM)
    hbm = pl.BlockSpec(memory_space=pl.ANY)
    dma = pltpu.SemaphoreType.DMA
    return pl.pallas_call(
        functools.partial(exit_kernel, slots=slots, groups=groups, angles=angles),
        name="exit_gradient",
        in_specs=[smem, smem, hbm, vmem, vmem, vmem, vmem],
        out_specs=[hbm, hbm],
        out_shape=[
            jax.ShapeDtypeStruct((2, groups, rows // 2, angles, tile_width), f32),
            jax.ShapeDtypeStruct((groups, angles, rows, tile_width), bf16),
        ],
        scratch_shapes=[
            pltpu.VMEM((angles, groups, rows, tile_width + side), bf16),
            pltpu.VMEM(((tile_width + side) // 128, n, 128), bf16),
            pltpu.VMEM((angles, groups, rows, tile_width), f32),
            pltpu.VMEM((angles, groups, rows, tile_width), bf16),
            pltpu.VMEM((n, slots * side), bf16),
            pltpu.VMEM((angles, groups, rows, side), bf16),
            pltpu.VMEM((angles, groups, rows, side), bf16),
            dma((angles,)),
            dma((angles, 2)),
            dma((angles,)),
            dma((2, angles)),
            dma((2, angles)),
            dma((angles, groups - 1)),
            dma((angles, groups - 1)),
        ],
        compiler_params=pltpu.CompilerParams(collective_id=2, has_side_effects=True),
    )(starts, counts, own, probe, amp, fwd, inv)


def back_kernel(ids, grad, tiles, out, *accs, feeds, pairs, angles):
    step = pl.program_id(0)
    owners, rows, width = out.shape
    blocks = accs[0].shape[0]

    @pl.when(step == 0)
    def _():
        def clear(i, carry):
            for acc in accs:
                acc[pl.ds(i * 8, 8)] = jnp.zeros((8, rows, 128), f32)
            return carry

        lax.fori_loop(0, blocks // 8, clear, 0)

    half = pairs * rows
    lo = low_half((half, 128))
    for a in range(angles):
        at = (step * angles + a) * (2 * pairs * feeds)
        flat = jnp.concatenate(
            [grad[0, a, :, bp * 128 : (bp + 1) * 128] for bp in range(pairs)], axis=0
        )
        zero = jnp.zeros_like(flat)
        halves = jnp.concatenate([jnp.where(lo, flat, zero), jnp.where(lo, zero, flat)], axis=0)
        twice = jnp.concatenate([tiles[a], tiles[a]], axis=0)
        contrib = jnp.dot(halves, twice, preferred_element_type=f32)
        for parity in range(2):
            for bp in range(pairs):
                first = at + (2 * bp + parity) * feeds
                top = (parity * pairs + bp) * rows
                where = [ids[first + j] for j in range(feeds)]
                old = [accs[j][where[j]] for j in range(feeds)]
                for j in range(feeds):
                    lane = j // 2 * 128
                    accs[j][where[j]] = old[j] + contrib[top : top + rows, lane : lane + 128]

    @pl.when(step == pl.num_programs(0) - 1)
    def _():
        lo = low_half((rows, 128))
        per_owner = width // 128

        def join(p, carry):
            at = pl.multiple_of(p * 128, 128)
            for o in range(owners):
                kb = 2 * (o * per_owner + p)
                even_lo = sum(accs[j][kb] for j in range(0, feeds, 2))
                even_hi = sum(accs[j][kb] for j in range(1, feeds, 2))
                odd_lo = sum(accs[j][kb + 1] for j in range(0, feeds, 2))
                odd_hi = sum(accs[j][kb + 1] for j in range(1, feeds, 2))
                joined = jnp.where(lo, even_lo, odd_hi) + pltpu.roll(
                    jnp.where(lo, odd_lo, even_hi), 64, 1
                )
                out[o, :, pl.ds(at, 128)] = joined.astype(bf16)
            return carry

        lax.fori_loop(0, per_owner, join, 0, unroll=2)


def back_project(ids, grad, tiles, owners, coefs):
    groups, angles, rows, tile_width = grad.shape
    angle_count, block, span = tiles.shape
    feeds = span // block
    dets = tile_width // block
    blocks = coefs // block
    width = coefs // owners
    return pl.pallas_call(
        functools.partial(back_kernel, feeds=feeds, pairs=dets // 2, angles=angles),
        name="back_project",
        out_shape=jax.ShapeDtypeStruct((owners, rows, width), bf16),
        grid_spec=pltpu.PrefetchScalarGridSpec(
            num_scalar_prefetch=1,
            grid=(groups,),
            in_specs=[
                pl.BlockSpec((1, angles, rows, tile_width), lambda g, ids: (g, 0, 0, 0)),
                pl.BlockSpec((angles, block, span), lambda g, ids: (g, 0, 0)),
            ],
            out_specs=pl.BlockSpec((owners, rows, width), lambda g, ids: (0, 0, 0)),
            scratch_shapes=[pltpu.VMEM((blocks, rows, 128), f32) for _ in range(feeds)],
        ),
    )(ids, grad, tiles)


def reduce_kernel(share, vol, out, near, mixed, far, send, recv):
    rows, width = vol.shape
    pos, partner, cross = pos_peers()
    beyond = lax.rem(partner + 2, 4)
    barrier = pltpu.get_barrier_semaphore()
    pl.semaphore_signal(barrier, inc=1, device_id={"pos": partner}, device_id_type=MESH)
    pl.semaphore_signal(barrier, inc=1, device_id={"pos": cross}, device_id_type=MESH)
    pl.semaphore_wait(barrier, 2)

    pieces = 4
    piece = width // pieces
    chunk = 512

    def columns(k):
        return pl.ds(k * piece, piece)

    def side(k):
        return remote(
            share.at[beyond, :, columns(k)], near.at[0, :, columns(k)], send.at[k], recv.at[k],
            {"pos": partner},
        )

    def over(k):
        return remote(
            mixed.at[:, columns(k)], far.at[:, columns(k)], send.at[pieces + k],
            recv.at[pieces + k], {"pos": cross},
        )

    home = remote(
        share.at[partner], near.at[1], send.at[2 * pieces], recv.at[2 * pieces], {"pos": partner}
    )
    for k in range(pieces):
        side(k).start()
    home.start()

    def mix(k):
        def body(i, carry):
            at = pl.ds(pl.multiple_of(k * piece + i * chunk, chunk), chunk)
            both = share[cross, :, at].astype(f32) + near[0, :, at].astype(f32)
            mixed[:, at] = both.astype(bf16)
            return carry

        lax.fori_loop(0, piece // chunk, body, 0)

    def total(k):
        def body(i, carry):
            at = pl.ds(pl.multiple_of(k * piece + i * chunk, chunk), chunk)
            both = share[pos, :, at].astype(f32) + near[1, :, at].astype(f32)
            out[:, at] = vol[:, at].astype(f32) + step_size * (both + far[:, at].astype(f32))
            return carry

        lax.fori_loop(0, piece // chunk, body, 0)

    for k in range(pieces):
        side(k).wait_recv()
        mix(k)
        if k > 0:
            over(k - 1).start()
    home.wait_recv()
    over(pieces - 1).start()
    for k in range(pieces):
        over(k).wait_recv()
        total(k)
    for k in range(pieces):
        side(k).wait_send()
        over(k).wait_send()
    home.wait_send()


def reduce_step(share, vol):
    rows, width = vol.shape
    vmem = pl.BlockSpec(memory_space=pltpu.VMEM)
    dma = pltpu.SemaphoreType.DMA
    return pl.pallas_call(
        reduce_kernel,
        name="reduce_step",
        out_shape=jax.ShapeDtypeStruct((rows, width), f32),
        in_specs=[vmem, vmem],
        out_specs=vmem,
        scratch_shapes=[
            pltpu.VMEM((2, rows, width), bf16),
            pltpu.VMEM((rows, width), bf16),
            pltpu.VMEM((rows, width), bf16),
            dma((9,)),
            dma((9,)),
        ],
        compiler_params=pltpu.CompilerParams(collective_id=1, has_side_effects=True),
    )(share, vol)


def on_device(volume, radon_tiles, tile_blocks, probe_field, amplitudes, offsets, counts):
    n_pos = lax.axis_size("pos")
    n_ang = lax.axis_size("ang")
    pos_index = lax.axis_index("pos")
    parts, slab, width = volume.shape
    block = radon_tiles.shape[1]
    own_blocks = tile_blocks.shape[1] // n_pos
    tile_width = own_blocks * block
    side = probe_field.shape[1]
    angles = amplitudes.shape[0]
    rows = parts * slab

    held = volume.reshape(rows, width)
    ids = lax.dynamic_slice_in_dim(tile_blocks, pos_index * own_blocks, own_blocks, 1).reshape(-1)
    cosine, sine_neg = dft_tables(side)
    fwd = jnp.concatenate(
        [jnp.concatenate([cosine, -sine_neg], 1), jnp.concatenate([sine_neg, cosine], 1)], 0
    )
    inv = jnp.concatenate(
        [jnp.concatenate([cosine, sine_neg], 1), jnp.concatenate([-sine_neg, cosine], 1)], 0
    )
    starts = offsets - pos_index * tile_width

    own = project(ids, held, radon_tiles, n_ang, n_pos)
    grad, back = exit_gradient(starts, counts, own, probe_field, amplitudes, fwd, inv)
    share = back_project(ids, back, radon_tiles, n_pos, n_pos * width)
    new_volume = reduce_step(share, held).reshape(volume.shape)
    proj_grad = grad.reshape(parts, n_ang * slab, angles, tile_width)
    return (new_volume, proj_grad)


def solution(mesh):
    in_specs = (
        P(None, "ang", "pos"),
        P(),
        P(),
        P(),
        P("ang", "pos", None, None),
        P("ang", "pos"),
        P("ang", "pos"),
    )
    out_specs = (P(None, "ang", "pos"), P(None, None, "ang", "pos"))
    return jax.shard_map(
        on_device, mesh=mesh, in_specs=in_specs, out_specs=out_specs, check_vma=False
    )
```

```python
import functools
import math

import jax
import jax.numpy as jnp
import numpy as np
from jax import lax
from jax.experimental import pallas as pl
from jax.experimental.pallas import tpu as pltpu
from jax.sharding import PartitionSpec as P

step_size = 0.1
f32 = jnp.float32
bf16 = jnp.bfloat16
MESH = pl.DeviceIdType.MESH


def dft_tables(width):
    index = np.arange(width, dtype=np.int32)
    phase = index[:, None] * index[None, :] % width
    turn = np.float32(2.0 * math.pi / width) * phase.astype(np.float32)
    cosine = (np.cos(turn) / np.float32(math.sqrt(width))).astype(bf16)
    sine_neg = (-np.sin(turn) / np.float32(math.sqrt(width))).astype(bf16)
    fwd = np.block([[cosine, -sine_neg], [sine_neg, cosine]])
    inv = np.block([[cosine, sine_neg], [-sine_neg, cosine]])
    return jnp.asarray(fwd), jnp.asarray(inv)


def low_half(shape):
    return lax.broadcasted_iota(jnp.int32, shape, len(shape) - 1) < 64


def pos_peers():
    pos = lax.axis_index("pos")
    partner = pos + 1 - 2 * lax.rem(pos, 2)
    cross = lax.rem(pos + 2, 4)
    return pos, partner, cross


def ang_peer(step, forward):
    me = lax.axis_index("ang")
    offset = lax.rem(13 * (step + 1), 32)
    way = 1 - 2 * lax.rem(lax.axis_index("pos"), 2)
    way = way if forward else -way
    z = lax.rem(lax.div(me, 8) + way * lax.div(offset, 8) + 4, 4)
    y = lax.rem(lax.rem(lax.div(me, 2), 4) + way * lax.rem(lax.div(offset, 2), 4) + 4, 4)
    x = lax.rem(lax.rem(me, 2) + lax.rem(offset, 2), 2)
    return z * 8 + y * 2 + x


def remote(src, dst, send_sem, recv_sem, device):
    return pltpu.make_async_remote_copy(
        src_ref=src,
        dst_ref=dst,
        send_sem=send_sem,
        recv_sem=recv_sem,
        device_id=device,
        device_id_type=MESH,
    )


def project_kernel(
    ids, vol, tiles_hbm, out, gathered, tiles, spread, ready, tile_sem, own_sem, pos_send, pos_recv,
    ang_send, ang_recv, *, feeds, pairs, angles, groups
):
    rows, width = vol.shape
    me = lax.axis_index("ang")
    pos, partner, cross = pos_peers()
    far = lax.rem(partner + 2, 4)
    load = pltpu.make_async_copy(tiles_hbm, tiles, tile_sem)
    load.start()

    barrier = pltpu.get_barrier_semaphore()
    pl.semaphore_signal(barrier, inc=1, device_id={"pos": partner}, device_id_type=MESH)
    pl.semaphore_signal(barrier, inc=1, device_id={"pos": cross}, device_id_type=MESH)

    def greet(step, carry):
        pl.semaphore_signal(
            barrier, inc=1, device_id={"ang": ang_peer(step, True)}, device_id_type=MESH
        )
        return carry

    lax.fori_loop(0, groups - 1, greet, 0)
    pl.semaphore_wait(barrier, groups + 1)

    to_cross = remote(vol, gathered.at[1], pos_send.at[1], pos_recv.at[1], {"pos": cross})
    to_partner = remote(vol, gathered.at[0], pos_send.at[0], pos_recv.at[0], {"pos": partner})
    onward = remote(
        gathered.at[1], gathered.at[2], pos_send.at[2], pos_recv.at[2], {"pos": partner}
    )
    to_cross.start()
    to_partner.start()

    lo32 = low_half((rows, 128))
    per_owner = width // 128

    def expand(source, owner):
        def body(p, carry):
            at = pl.multiple_of(p * 128, 128)
            tile = source[:, pl.ds(at, 128)].astype(f32)
            turned = pltpu.roll(tile, 64, 1)
            base = 2 * (owner * per_owner + p)
            spread[base] = jnp.where(lo32, tile, turned).astype(bf16)
            spread[base + 1] = jnp.where(lo32, turned, tile).astype(bf16)
            return carry

        lax.fori_loop(0, per_owner, body, 0, unroll=4)

    expand(vol, pos)
    to_partner.wait_recv()
    expand(gathered.at[0], partner)
    to_cross.wait_recv()
    onward.start()
    expand(gathered.at[1], cross)
    load.wait()
    onward.wait_recv()
    expand(gathered.at[2], far)

    def outgoing(step):
        group = ang_peer(step, True)
        return remote(
            ready.at[group], out.at[me], ang_send.at[step], ang_recv.at[step], {"ang": group}
        )

    def incoming(step):
        group = ang_peer(step, False)
        return remote(
            ready.at[group], out.at[group], ang_send.at[step], ang_recv.at[step], {"ang": group}
        )

    lo = low_half((rows, 128))
    half = pairs * rows
    lo_half = low_half((half, 128))
    total = groups * angles

    def group_step(step, carry):
        @pl.when(step > 0)
        def _():
            outgoing(step - 1).start()

        group = ang_peer(step, True)
        for a in range(angles):
            at = group * angles + a
            halves = []
            for parity in range(2):
                for bp in range(pairs):
                    first = (2 * bp + parity) * feeds
                    tile = [spread[ids[(first + j) * total + at]] for j in range(feeds)]
                    halves.append(
                        jnp.concatenate(
                            [jnp.where(lo, tile[j], tile[j + 1]) for j in range(0, feeds, 2)],
                            axis=1,
                        )
                    )
            picked = jnp.concatenate(halves, axis=0)
            radon = tiles[group * angles + a]
            twice = jnp.concatenate([radon, radon], axis=0)
            both = lax.dot_general(
                picked, twice, (((1,), (1,)), ((), ())), preferred_element_type=f32
            )
            joined = jnp.where(lo_half, both[:half], both[half:]).astype(bf16)
            for bp in range(pairs):
                ready[group, a, :, bp * 128 : (bp + 1) * 128] = joined[bp * rows : (bp + 1) * rows]
        return carry

    lax.fori_loop(0, groups, group_step, 0)
    to_cross.wait_send()
    to_partner.wait_send()
    onward.wait_send()
    mine = pltpu.make_async_copy(ready.at[me], out.at[me], own_sem)
    mine.start()

    def finish(step, carry):
        outgoing(step).wait_send()
        incoming(step).wait_recv()
        return carry

    lax.fori_loop(0, groups - 1, finish, 0)
    mine.wait()


def project(ids, vol, tiles, groups, owners):
    rows, width = vol.shape
    angle_count, block, span = tiles.shape
    feeds = span // block
    per_angle = ids.shape[0] // angle_count
    dets = per_angle // feeds
    angles = angle_count // groups
    blocks = owners * width // block
    dma = pltpu.SemaphoreType.DMA
    return pl.pallas_call(
        functools.partial(
            project_kernel, feeds=feeds, pairs=dets // 2, angles=angles, groups=groups
        ),
        name="project",
        out_shape=jax.ShapeDtypeStruct((groups, angles, rows, dets * block), bf16),
        in_specs=[
            pl.BlockSpec(memory_space=pltpu.SMEM),
            pl.BlockSpec(memory_space=pltpu.VMEM),
            pl.BlockSpec(memory_space=pl.ANY),
        ],
        out_specs=pl.BlockSpec(memory_space=pl.ANY),
        scratch_shapes=[
            pltpu.VMEM((owners - 1, rows, width), bf16),
            pltpu.VMEM(tiles.shape, bf16),
            pltpu.VMEM((blocks, rows, 128), bf16),
            pltpu.VMEM((groups, angles, rows, dets * block), bf16),
            dma,
            dma,
            dma((3,)),
            dma((3,)),
            dma((groups - 1,)),
            dma((groups - 1,)),
        ],
        compiler_params=pltpu.CompilerParams(collective_id=0, has_side_effects=True),
    )(ids, vol, tiles)


def exit_kernel(
    starts, counts, own, probe, amp, fwd, inv, grad, back, landed, strip, summed, rounded, patches,
    spill_out, spill_in, load_sem, store_sem, own_sem, pos_send, pos_recv, ang_send, ang_recv,
    *, slots, groups, angles
):
    rows, tile_width = own.shape[2:]
    side = probe.shape[1]
    n = groups * rows
    me = lax.axis_index("ang")
    pos = lax.axis_index("pos")
    after = lax.rem(pos + 1, 4)
    before = lax.rem(pos + 3, 4)

    def load(a):
        return pltpu.make_async_copy(
            own.at[:, a], landed.at[a, :, :, :tile_width], load_sem.at[a]
        )

    def halo(a):
        return remote(
            own.at[:, a, :, :side], landed.at[a, :, :, tile_width:], pos_send.at[0, a],
            pos_recv.at[0, a], {"pos": before},
        )

    def spill(a):
        return remote(
            spill_out.at[a], spill_in.at[a], pos_send.at[1, a], pos_recv.at[1, a], {"pos": after}
        )

    parts = (slice(0, side), slice(side, tile_width))

    def outgoing(a, h, step):
        group = ang_peer(step, True)
        return remote(
            rounded.at[a, group, :, parts[h]], back.at[me, a, :, parts[h]],
            ang_send.at[a, h, step], ang_recv.at[a, h, step], {"ang": group},
        )

    def incoming(a, h, step):
        group = ang_peer(step, False)
        return remote(
            rounded.at[a, group, :, parts[h]], back.at[group, a, :, parts[h]],
            ang_send.at[a, h, step], ang_recv.at[a, h, step], {"ang": group},
        )

    def depart(a, h):
        def body(step, carry):
            outgoing(a, h, step).start()
            return carry

        lax.fori_loop(0, groups - 1, body, 0)

    def keep(a):
        return pltpu.make_async_copy(rounded.at[a, me], back.at[me, a], own_sem.at[a])

    def store(a, c):
        half = rows // 2
        return pltpu.make_async_copy(
            summed.at[a, :, c * half : (c + 1) * half], grad.at[c, :, :, a, :], store_sem.at[a, c]
        )

    for a in range(angles):
        load(a).start()
    barrier = pltpu.get_barrier_semaphore()
    pl.semaphore_signal(barrier, inc=1, device_id={"pos": before}, device_id_type=MESH)
    pl.semaphore_signal(barrier, inc=1, device_id={"pos": after}, device_id_type=MESH)

    def greet(step, carry):
        pl.semaphore_signal(
            barrier, inc=1, device_id={"ang": ang_peer(step, True)}, device_id_type=MESH
        )
        return carry

    lax.fori_loop(0, groups - 1, greet, 0)
    pl.semaphore_wait(barrier, groups + 1)
    for a in range(angles):
        halo(a).start()

    window = side + 128
    probe_re = probe[0].astype(f32)
    probe_im = probe[1].astype(f32)

    def compute(a):
        load(a).wait()
        halo(a).wait_recv()
        for lane in range((tile_width + side) // 128):
            part = landed[a, :, :, lane * 128 : (lane + 1) * 128]
            strip[lane] = part.reshape(n, 128)
        for slot in range(slots):
            start = lax.rem(starts[a, slot], tile_width)
            block = lax.div(start, 128)
            shift = start - block * 128
            source = lax.broadcasted_iota(jnp.int32, (window, side), 0)
            target = lax.broadcasted_iota(jnp.int32, (window, side), 1)
            pick = jnp.where(source - target == shift, 1.0, 0.0).astype(bf16)
            view = jnp.concatenate([strip[block + i] for i in range(window // 128)], axis=1)
            patch = jnp.dot(view, pick, preferred_element_type=f32)
            patch = patch.reshape(groups, 2, rows // 2, side)
            patch_re = patch[:, 0].reshape(side, side)
            patch_im = patch[:, 1].reshape(side, side)
            wave_re = (probe_re * patch_re - probe_im * patch_im).astype(bf16)
            wave_im = (probe_re * patch_im + probe_im * patch_re).astype(bf16)
            wave = jnp.concatenate([wave_re, wave_im], axis=0)
            half = jnp.dot(fwd[...], wave, preferred_element_type=f32).astype(bf16)
            half = jnp.concatenate([half[:side], half[side:]], axis=1)
            far = jnp.dot(half, inv[...], preferred_element_type=f32)
            far_re = far[:, :side]
            far_im = far[:, side:]
            power = far_re * far_re + far_im * far_im
            factor = amp[a, slot].astype(f32) * lax.rsqrt(jnp.maximum(power, 1.0)) - 1.0
            delta = jnp.concatenate(
                [(far_re * factor).astype(bf16), (far_im * factor).astype(bf16)], axis=0
            )
            turned = jnp.dot(inv[...], delta, preferred_element_type=f32).astype(bf16)
            turned = jnp.concatenate([turned[:side], turned[side:]], axis=1)
            near = jnp.dot(turned, fwd[...], preferred_element_type=f32)
            near_re = near[:, :side]
            near_im = near[:, side:]
            live = jnp.minimum(jnp.maximum(counts[a] - slot, 0), 1).astype(f32)
            grad_re = (probe_re * near_re + probe_im * near_im) * live
            grad_im = (probe_re * near_im - probe_im * near_re) * live
            both = jnp.concatenate(
                [
                    grad_re.reshape(groups, 1, rows // 2, side),
                    grad_im.reshape(groups, 1, rows // 2, side),
                ],
                axis=1,
            ).reshape(n, side)
            patches[:, slot * side : (slot + 1) * side] = both.astype(bf16)
            if slot == slots - 2:

                @pl.when(a > 0)
                def _():
                    send(a - 1)

        whole = tile_width + side
        source = lax.broadcasted_iota(jnp.int32, (side, whole), 1)
        target = lax.broadcasted_iota(jnp.int32, (side, whole), 0)
        place = jnp.concatenate(
            [
                jnp.where(source - target == lax.rem(starts[a, slot], tile_width), 1.0, 0.0).astype(bf16)
                for slot in range(slots)
            ],
            axis=0,
        )
        over = jnp.dot(patches[...], place[:, tile_width:], preferred_element_type=f32)
        spill_out[a] = over.astype(bf16).reshape(groups, rows, side)
        inside = jnp.dot(patches[...], place[:, :tile_width], preferred_element_type=f32)
        spill(a).start()
        rounded[a, :, :, side:] = inside[:, side:].astype(bf16).reshape(
            groups, rows, tile_width - side
        )
        summed[a] = inside.reshape(groups, rows, tile_width)
        depart(a, 1)

    def send(a):
        spill(a).wait_recv()

        def body(g, carry):
            left = summed[a, g, :, :side] + spill_in[a, g].astype(f32)
            summed[a, g, :, :side] = left
            rounded[a, g, :, :side] = left.astype(bf16)
            return carry

        lax.fori_loop(0, groups, body, 0, unroll=2)
        for c in range(2):
            store(a, c).start()
        depart(a, 0)
        keep(a).start()

    def angle_step(a, carry):
        compute(a)
        return carry

    lax.fori_loop(0, angles, angle_step, 0)
    send(angles - 1)
    for a in range(angles):
        halo(a).wait_send()
        spill(a).wait_send()
        keep(a).wait()
        for c in range(2):
            store(a, c).wait()

    def finish(step, carry):
        for a in range(angles):
            for h in range(2):
                outgoing(a, h, step).wait_send()
                incoming(a, h, step).wait_recv()
        return carry

    lax.fori_loop(0, groups - 1, finish, 0)


def exit_gradient(starts, counts, own, probe, amp, fwd, inv):
    groups, angles, rows, tile_width = own.shape
    side = probe.shape[1]
    slots = starts.shape[1]
    n = groups * rows
    smem = pl.BlockSpec(memory_space=pltpu.SMEM)
    vmem = pl.BlockSpec(memory_space=pltpu.VMEM)
    hbm = pl.BlockSpec(memory_space=pl.ANY)
    dma = pltpu.SemaphoreType.DMA
    return pl.pallas_call(
        functools.partial(exit_kernel, slots=slots, groups=groups, angles=angles),
        name="exit_gradient",
        in_specs=[smem, smem, hbm, vmem, vmem, vmem, vmem],
        out_specs=[hbm, hbm],
        out_shape=[
            jax.ShapeDtypeStruct((2, groups, rows // 2, angles, tile_width), f32),
            jax.ShapeDtypeStruct((groups, angles, rows, tile_width), bf16),
        ],
        scratch_shapes=[
            pltpu.VMEM((angles, groups, rows, tile_width + side), bf16),
            pltpu.VMEM(((tile_width + side) // 128, n, 128), bf16),
            pltpu.VMEM((angles, groups, rows, tile_width), f32),
            pltpu.VMEM((angles, groups, rows, tile_width), bf16),
            pltpu.VMEM((n, slots * side), bf16),
            pltpu.VMEM((angles, groups, rows, side), bf16),
            pltpu.VMEM((angles, groups, rows, side), bf16),
            dma((angles,)),
            dma((angles, 2)),
            dma((angles,)),
            dma((2, angles)),
            dma((2, angles)),
            dma((angles, 2, groups - 1)),
            dma((angles, 2, groups - 1)),
        ],
        compiler_params=pltpu.CompilerParams(collective_id=2, has_side_effects=True),
    )(starts, counts, own, probe, amp, fwd, inv)


def back_kernel(ids, grad, tiles, exact, out, kept, *scratch, feeds, pairs, angles):
    step = pl.program_id(0)
    accs = scratch[:-1]
    total = pl.num_programs(0) * angles
    keep = pltpu.make_async_copy(exact, kept.at[:, pl.ds(step, 1)], scratch[-1])
    keep.start()
    owners, rows, width = out.shape
    blocks = accs[0].shape[0]

    @pl.when(step == 0)
    def _():
        def clear(i, carry):
            for acc in accs:
                acc[pl.ds(i * 8, 8)] = jnp.zeros((8, rows, 128), f32)
            return carry

        lax.fori_loop(0, blocks // 8, clear, 0)

    half = pairs * rows
    lo = low_half((half, 128))
    for a in range(angles):
        at = step * angles + a
        flat = jnp.concatenate(
            [grad[0, a, :, bp * 128 : (bp + 1) * 128] for bp in range(pairs)], axis=0
        )
        zero = jnp.zeros_like(flat)
        halves = jnp.concatenate([jnp.where(lo, flat, zero), jnp.where(lo, zero, flat)], axis=0)
        twice = jnp.concatenate([tiles[a], tiles[a]], axis=0)
        contrib = jnp.dot(halves, twice, preferred_element_type=f32)
        for parity in range(2):
            for bp in range(pairs):
                first = (2 * bp + parity) * feeds
                top = (parity * pairs + bp) * rows
                where = [ids[(first + j) * total + at] for j in range(feeds)]
                old = [accs[j][where[j]] for j in range(feeds)]
                for j in range(feeds):
                    lane = j // 2 * 128
                    accs[j][where[j]] = old[j] + contrib[top : top + rows, lane : lane + 128]

    keep.wait()

    @pl.when(step == pl.num_programs(0) - 1)
    def _():
        lo = low_half((rows, 128))
        per_owner = width // 128

        def join(p, carry):
            at = pl.multiple_of(p * 128, 128)
            for o in range(owners):
                kb = 2 * (o * per_owner + p)
                even_lo = sum(accs[j][kb] for j in range(0, feeds, 2))
                even_hi = sum(accs[j][kb] for j in range(1, feeds, 2))
                odd_lo = sum(accs[j][kb + 1] for j in range(0, feeds, 2))
                odd_hi = sum(accs[j][kb + 1] for j in range(1, feeds, 2))
                joined = jnp.where(lo, even_lo, odd_hi) + pltpu.roll(
                    jnp.where(lo, odd_lo, even_hi), 64, 1
                )
                out[o, :, pl.ds(at, 128)] = joined.astype(bf16)
            return carry

        lax.fori_loop(0, per_owner, join, 0, unroll=2)


def back_project(ids, grad, tiles, exact, owners, coefs):
    groups, angles, rows, tile_width = grad.shape
    angle_count, block, span = tiles.shape
    feeds = span // block
    dets = tile_width // block
    blocks = coefs // block
    width = coefs // owners
    return pl.pallas_call(
        functools.partial(back_kernel, feeds=feeds, pairs=dets // 2, angles=angles),
        name="back_project",
        out_shape=[
            jax.ShapeDtypeStruct((owners, rows, width), bf16),
            jax.ShapeDtypeStruct(exact.shape, f32),
        ],
        grid_spec=pltpu.PrefetchScalarGridSpec(
            num_scalar_prefetch=1,
            grid=(groups,),
            in_specs=[
                pl.BlockSpec((1, angles, rows, tile_width), lambda g, ids: (g, 0, 0, 0)),
                pl.BlockSpec((angles, block, span), lambda g, ids: (g, 0, 0)),
                pl.BlockSpec((2, 1, rows // 2, angles, tile_width), lambda g, ids: (0, g, 0, 0, 0)),
            ],
            out_specs=[
                pl.BlockSpec((owners, rows, width), lambda g, ids: (0, 0, 0)),
                pl.BlockSpec(memory_space=pl.ANY),
            ],
            scratch_shapes=[pltpu.VMEM((blocks, rows, 128), f32) for _ in range(feeds)]
            + [pltpu.SemaphoreType.DMA],
        ),
    )(ids, grad, tiles, exact)


def reduce_kernel(share, vol, out, near, mixed, far, send, recv):
    rows, width = vol.shape
    pos, partner, cross = pos_peers()
    beyond = lax.rem(partner + 2, 4)
    barrier = pltpu.get_barrier_semaphore()
    pl.semaphore_signal(barrier, inc=1, device_id={"pos": partner}, device_id_type=MESH)
    pl.semaphore_signal(barrier, inc=1, device_id={"pos": cross}, device_id_type=MESH)
    pl.semaphore_wait(barrier, 2)

    pieces = 4
    piece = width // pieces
    chunk = 512

    def columns(k):
        return pl.ds(k * piece, piece)

    def side(k):
        return remote(
            share.at[beyond, :, columns(k)], near.at[0, :, columns(k)], send.at[k], recv.at[k],
            {"pos": partner},
        )

    def over(k):
        return remote(
            mixed.at[:, columns(k)], far.at[:, columns(k)], send.at[pieces + k],
            recv.at[pieces + k], {"pos": cross},
        )

    home = remote(
        share.at[partner], near.at[1], send.at[2 * pieces], recv.at[2 * pieces], {"pos": partner}
    )
    for k in range(pieces):
        side(k).start()
    home.start()

    def mix(k):
        def body(i, carry):
            at = pl.ds(pl.multiple_of(k * piece + i * chunk, chunk), chunk)
            both = share[cross, :, at].astype(f32) + near[0, :, at].astype(f32)
            mixed[:, at] = both.astype(bf16)
            return carry

        lax.fori_loop(0, piece // chunk, body, 0)

    def total(k):
        def body(i, carry):
            at = pl.ds(pl.multiple_of(k * piece + i * chunk, chunk), chunk)
            both = share[pos, :, at].astype(f32) + near[1, :, at].astype(f32)
            out[:, at] = vol[:, at].astype(f32) + step_size * (both + far[:, at].astype(f32))
            return carry

        lax.fori_loop(0, piece // chunk, body, 0)

    for k in range(pieces):
        side(k).wait_recv()
        mix(k)
        if k > 0:
            over(k - 1).start()
    home.wait_recv()
    over(pieces - 1).start()
    for k in range(pieces):
        over(k).wait_recv()
        total(k)
    for k in range(pieces):
        side(k).wait_send()
        over(k).wait_send()
    home.wait_send()


def reduce_step(share, vol):
    rows, width = vol.shape
    vmem = pl.BlockSpec(memory_space=pltpu.VMEM)
    dma = pltpu.SemaphoreType.DMA
    return pl.pallas_call(
        reduce_kernel,
        name="reduce_step",
        out_shape=jax.ShapeDtypeStruct((rows, width), f32),
        in_specs=[vmem, vmem],
        out_specs=vmem,
        scratch_shapes=[
            pltpu.VMEM((2, rows, width), bf16),
            pltpu.VMEM((rows, width), bf16),
            pltpu.VMEM((rows, width), bf16),
            dma((9,)),
            dma((9,)),
        ],
        compiler_params=pltpu.CompilerParams(collective_id=1, has_side_effects=True),
    )(share, vol)


def on_device(volume, radon_tiles, tile_blocks, probe_field, amplitudes, offsets, counts):
    n_pos = lax.axis_size("pos")
    n_ang = lax.axis_size("ang")
    pos_index = lax.axis_index("pos")
    parts, slab, width = volume.shape
    block = radon_tiles.shape[1]
    own_blocks = tile_blocks.shape[1] // n_pos
    tile_width = own_blocks * block
    side = probe_field.shape[1]
    angles = amplitudes.shape[0]
    rows = parts * slab

    held = volume.reshape(rows, width)
    by_angle = tile_blocks.transpose(1, 2, 0)
    ids = lax.dynamic_slice_in_dim(by_angle, pos_index * own_blocks, own_blocks, 0).reshape(-1)
    fwd, inv = dft_tables(side)
    own = project(ids, held, radon_tiles, n_ang, n_pos)
    grad, back = exit_gradient(offsets, counts.reshape(-1), own, probe_field, amplitudes, fwd, inv)
    share, kept = back_project(ids, back, radon_tiles, grad, n_pos, n_pos * width)
    new_volume = reduce_step(share, held).reshape(volume.shape)
    proj_grad = kept.reshape(parts, n_ang * slab, angles, tile_width)
    return (new_volume, proj_grad)


def solution(mesh):
    in_specs = (
        P(None, "ang", "pos"),
        P(),
        P(),
        P(),
        P("ang", "pos", None, None),
        P("ang", "pos"),
        P("ang", "pos"),
    )
    out_specs = (P(None, "ang", "pos"), P(None, None, "ang", "pos"))
    return jax.shard_map(
        on_device, mesh=mesh, in_specs=in_specs, out_specs=out_specs, check_vma=False
    )
```

```python
import functools
import math

import jax
import jax.numpy as jnp
import numpy as np
from jax import lax
from jax.experimental import pallas as pl
from jax.experimental.pallas import tpu as pltpu
from jax.sharding import PartitionSpec as P

step_size = 0.1
f32 = jnp.float32
bf16 = jnp.bfloat16
MESH = pl.DeviceIdType.MESH


def dft_tables(width):
    index = np.arange(width, dtype=np.int32)
    phase = index[:, None] * index[None, :] % width
    turn = np.float32(2.0 * math.pi / width) * phase.astype(np.float32)
    cosine = (np.cos(turn) / np.float32(math.sqrt(width))).astype(bf16)
    sine_neg = (-np.sin(turn) / np.float32(math.sqrt(width))).astype(bf16)
    fwd = np.block([[cosine, -sine_neg], [sine_neg, cosine]])
    inv = np.block([[cosine, sine_neg], [-sine_neg, cosine]])
    return jnp.asarray(fwd), jnp.asarray(inv)


def low_half(shape):
    return lax.broadcasted_iota(jnp.int32, shape, len(shape) - 1) < 64


def pos_peers():
    pos = lax.axis_index("pos")
    partner = pos + 1 - 2 * lax.rem(pos, 2)
    cross = lax.rem(pos + 2, 4)
    return pos, partner, cross


def ang_peer(step, forward):
    me = lax.axis_index("ang")
    offset = lax.rem(13 * (step + 1), 32)
    way = 1 - 2 * lax.rem(lax.axis_index("pos"), 2)
    way = way if forward else -way
    z = lax.rem(lax.div(me, 8) + way * lax.div(offset, 8) + 4, 4)
    y = lax.rem(lax.rem(lax.div(me, 2), 4) + way * lax.rem(lax.div(offset, 2), 4) + 4, 4)
    x = lax.rem(lax.rem(me, 2) + lax.rem(offset, 2), 2)
    return z * 8 + y * 2 + x


def remote(src, dst, send_sem, recv_sem, device):
    return pltpu.make_async_remote_copy(
        src_ref=src,
        dst_ref=dst,
        send_sem=send_sem,
        recv_sem=recv_sem,
        device_id=device,
        device_id_type=MESH,
    )


def project_kernel(
    ids, vol, tiles_hbm, out, gathered, tiles, spread, ready, tile_sem, own_sem, pos_send, pos_recv,
    ang_send, ang_recv, *, feeds, pairs, angles, groups
):
    rows, width = vol.shape
    me = lax.axis_index("ang")
    pos, partner, cross = pos_peers()
    far = lax.rem(partner + 2, 4)
    load = pltpu.make_async_copy(tiles_hbm, tiles, tile_sem)
    load.start()

    barrier = pltpu.get_barrier_semaphore()
    pl.semaphore_signal(barrier, inc=1, device_id={"pos": partner}, device_id_type=MESH)
    pl.semaphore_signal(barrier, inc=1, device_id={"pos": cross}, device_id_type=MESH)

    def greet(step, carry):
        pl.semaphore_signal(
            barrier, inc=1, device_id={"ang": ang_peer(step, True)}, device_id_type=MESH
        )
        return carry

    lax.fori_loop(0, groups - 1, greet, 0)
    pl.semaphore_wait(barrier, groups + 1)

    to_cross = remote(vol, gathered.at[1], pos_send.at[1], pos_recv.at[1], {"pos": cross})
    to_partner = remote(vol, gathered.at[0], pos_send.at[0], pos_recv.at[0], {"pos": partner})
    onward = remote(
        gathered.at[1], gathered.at[2], pos_send.at[2], pos_recv.at[2], {"pos": partner}
    )
    to_cross.start()
    to_partner.start()

    lo32 = low_half((rows, 128))
    per_owner = width // 128

    def expand(source, owner):
        def body(p, carry):
            at = pl.multiple_of(p * 128, 128)
            tile = source[:, pl.ds(at, 128)].astype(f32)
            turned = pltpu.roll(tile, 64, 1)
            base = 2 * (owner * per_owner + p)
            spread[base] = jnp.where(lo32, tile, turned).astype(bf16)
            spread[base + 1] = jnp.where(lo32, turned, tile).astype(bf16)
            return carry

        lax.fori_loop(0, per_owner, body, 0, unroll=4)

    expand(vol, pos)
    to_partner.wait_recv()
    expand(gathered.at[0], partner)
    to_cross.wait_recv()
    onward.start()
    expand(gathered.at[1], cross)
    load.wait()
    onward.wait_recv()
    expand(gathered.at[2], far)

    def outgoing(step):
        group = ang_peer(step, True)
        return remote(
            ready.at[group], out.at[me], ang_send.at[step], ang_recv.at[step], {"ang": group}
        )

    def incoming(step):
        group = ang_peer(step, False)
        return remote(
            ready.at[group], out.at[group], ang_send.at[step], ang_recv.at[step], {"ang": group}
        )

    lo = low_half((rows, 128))
    half = pairs * rows
    lo_half = low_half((half, 128))
    total = groups * angles

    def group_step(step, carry):
        @pl.when(step > 0)
        def _():
            outgoing(step - 1).start()

        group = ang_peer(step, True)
        for a in range(angles):
            at = group * angles + a
            halves = []
            for parity in range(2):
                for bp in range(pairs):
                    first = (2 * bp + parity) * feeds
                    tile = [spread[ids[(first + j) * total + at]] for j in range(feeds)]
                    halves.append(
                        jnp.concatenate(
                            [jnp.where(lo, tile[j], tile[j + 1]) for j in range(0, feeds, 2)],
                            axis=1,
                        )
                    )
            picked = jnp.concatenate(halves, axis=0)
            radon = tiles[group * angles + a]
            twice = jnp.concatenate([radon, radon], axis=0)
            both = lax.dot_general(
                picked, twice, (((1,), (1,)), ((), ())), preferred_element_type=f32
            )
            joined = jnp.where(lo_half, both[:half], both[half:]).astype(bf16)
            for bp in range(pairs):
                ready[group, a, :, bp * 128 : (bp + 1) * 128] = joined[bp * rows : (bp + 1) * rows]
        return carry

    lax.fori_loop(0, groups, group_step, 0)
    to_cross.wait_send()
    to_partner.wait_send()
    onward.wait_send()
    mine = pltpu.make_async_copy(ready.at[me], out.at[me], own_sem)
    mine.start()

    def finish(step, carry):
        outgoing(step).wait_send()
        incoming(step).wait_recv()
        return carry

    lax.fori_loop(0, groups - 1, finish, 0)
    mine.wait()


def project(ids, vol, tiles, groups, owners):
    rows, width = vol.shape
    angle_count, block, span = tiles.shape
    feeds = span // block
    per_angle = ids.shape[0] // angle_count
    dets = per_angle // feeds
    angles = angle_count // groups
    blocks = owners * width // block
    dma = pltpu.SemaphoreType.DMA
    return pl.pallas_call(
        functools.partial(
            project_kernel, feeds=feeds, pairs=dets // 2, angles=angles, groups=groups
        ),
        name="project",
        out_shape=jax.ShapeDtypeStruct((groups, angles, rows, dets * block), bf16),
        in_specs=[
            pl.BlockSpec(memory_space=pltpu.SMEM),
            pl.BlockSpec(memory_space=pltpu.VMEM),
            pl.BlockSpec(memory_space=pl.ANY),
        ],
        out_specs=pl.BlockSpec(memory_space=pl.ANY),
        scratch_shapes=[
            pltpu.VMEM((owners - 1, rows, width), bf16),
            pltpu.VMEM(tiles.shape, bf16),
            pltpu.VMEM((blocks, rows, 128), bf16),
            pltpu.VMEM((groups, angles, rows, dets * block), bf16),
            dma,
            dma,
            dma((3,)),
            dma((3,)),
            dma((groups - 1,)),
            dma((groups - 1,)),
        ],
        compiler_params=pltpu.CompilerParams(collective_id=0, has_side_effects=True),
    )(ids, vol, tiles)


def exit_kernel(
    starts, counts, own, probe, amp, fwd, inv, grad, back, landed, strip, summed, rounded, patches,
    spill_out, spill_in, load_sem, store_sem, own_sem, pos_send, pos_recv, ang_send, ang_recv,
    *, slots, groups, angles
):
    rows, tile_width = own.shape[2:]
    side = probe.shape[1]
    n = groups * rows
    me = lax.axis_index("ang")
    pos = lax.axis_index("pos")
    after = lax.rem(pos + 1, 4)
    before = lax.rem(pos + 3, 4)

    def load(a):
        return pltpu.make_async_copy(
            own.at[:, a], landed.at[a, :, :, :tile_width], load_sem.at[a]
        )

    def halo(a):
        return remote(
            own.at[:, a, :, :side], landed.at[a, :, :, tile_width:], pos_send.at[0, a],
            pos_recv.at[0, a], {"pos": before},
        )

    def spill(a):
        return remote(
            spill_out.at[a], spill_in.at[a], pos_send.at[1, a], pos_recv.at[1, a], {"pos": after}
        )

    parts = (slice(0, side), slice(side, tile_width))

    def outgoing(a, h, step):
        group = ang_peer(step, True)
        return remote(
            rounded.at[a, group, :, parts[h]], back.at[me, a, :, parts[h]],
            ang_send.at[a, h, step], ang_recv.at[a, h, step], {"ang": group},
        )

    def incoming(a, h, step):
        group = ang_peer(step, False)
        return remote(
            rounded.at[a, group, :, parts[h]], back.at[group, a, :, parts[h]],
            ang_send.at[a, h, step], ang_recv.at[a, h, step], {"ang": group},
        )

    def depart(a, h):
        def body(step, carry):
            outgoing(a, h, step).start()
            return carry

        lax.fori_loop(0, groups - 1, body, 0)

    def keep(a):
        return pltpu.make_async_copy(rounded.at[a, me], back.at[me, a], own_sem.at[a])

    def store(a, c):
        half = rows // 2
        return pltpu.make_async_copy(
            summed.at[a, :, c * half : (c + 1) * half], grad.at[c, :, :, a, :], store_sem.at[a, c]
        )

    for a in range(angles):
        load(a).start()
    barrier = pltpu.get_barrier_semaphore()
    pl.semaphore_signal(barrier, inc=1, device_id={"pos": before}, device_id_type=MESH)
    pl.semaphore_signal(barrier, inc=1, device_id={"pos": after}, device_id_type=MESH)

    def greet(step, carry):
        pl.semaphore_signal(
            barrier, inc=1, device_id={"ang": ang_peer(step, True)}, device_id_type=MESH
        )
        return carry

    lax.fori_loop(0, groups - 1, greet, 0)
    pl.semaphore_wait(barrier, groups + 1)
    for a in range(angles):
        halo(a).start()

    window = side + 128
    probe_re = probe[0].astype(f32)
    probe_im = probe[1].astype(f32)

    def compute(a):
        load(a).wait()
        halo(a).wait_recv()
        for lane in range((tile_width + side) // 128):
            part = landed[a, :, :, lane * 128 : (lane + 1) * 128]
            strip[lane] = part.reshape(n, 128)
        for slot in range(slots):
            start = lax.rem(starts[a, slot], tile_width)
            block = lax.div(start, 128)
            shift = start - block * 128
            source = lax.broadcasted_iota(jnp.int32, (window, side), 0)
            target = lax.broadcasted_iota(jnp.int32, (window, side), 1)
            pick = jnp.where(source - target == shift, 1.0, 0.0).astype(bf16)
            view = jnp.concatenate([strip[block + i] for i in range(window // 128)], axis=1)
            patch = jnp.dot(view, pick, preferred_element_type=f32)
            patch = patch.reshape(groups, 2, rows // 2, side)
            patch_re = patch[:, 0].reshape(side, side)
            patch_im = patch[:, 1].reshape(side, side)
            wave_re = (probe_re * patch_re - probe_im * patch_im).astype(bf16)
            wave_im = (probe_re * patch_im + probe_im * patch_re).astype(bf16)
            wave = jnp.concatenate([wave_re, wave_im], axis=0)
            half = jnp.dot(fwd[...], wave, preferred_element_type=f32).astype(bf16)
            half = jnp.concatenate([half[:side], half[side:]], axis=1)
            far = jnp.dot(half, inv[...], preferred_element_type=f32)
            far_re = far[:, :side]
            far_im = far[:, side:]
            power = far_re * far_re + far_im * far_im
            factor = amp[a, slot].astype(f32) * lax.rsqrt(jnp.maximum(power, 1.0)) - 1.0
            delta = jnp.concatenate(
                [(far_re * factor).astype(bf16), (far_im * factor).astype(bf16)], axis=0
            )
            turned = jnp.dot(inv[...], delta, preferred_element_type=f32).astype(bf16)
            turned = jnp.concatenate([turned[:side], turned[side:]], axis=1)
            near = jnp.dot(turned, fwd[...], preferred_element_type=f32)
            near_re = near[:, :side]
            near_im = near[:, side:]
            live = jnp.minimum(jnp.maximum(counts[a] - slot, 0), 1).astype(f32)
            grad_re = (probe_re * near_re + probe_im * near_im) * live
            grad_im = (probe_re * near_im - probe_im * near_re) * live
            both = jnp.concatenate(
                [
                    grad_re.reshape(groups, 1, rows // 2, side),
                    grad_im.reshape(groups, 1, rows // 2, side),
                ],
                axis=1,
            ).reshape(n, side)
            patches[:, slot * side : (slot + 1) * side] = both.astype(bf16)
            if slot == slots - 2:

                @pl.when(a > 0)
                def _():
                    send(a - 1)

        whole = tile_width + side
        source = lax.broadcasted_iota(jnp.int32, (side, whole), 1)
        target = lax.broadcasted_iota(jnp.int32, (side, whole), 0)
        place = jnp.concatenate(
            [
                jnp.where(source - target == lax.rem(starts[a, slot], tile_width), 1.0, 0.0).astype(bf16)
                for slot in range(slots)
            ],
            axis=0,
        )
        over = jnp.dot(patches[...], place[:, tile_width:], preferred_element_type=f32)
        spill_out[a] = over.astype(bf16).reshape(groups, rows, side)
        inside = jnp.dot(patches[...], place[:, :tile_width], preferred_element_type=f32)
        spill(a).start()
        rounded[a, :, :, side:] = inside[:, side:].astype(bf16).reshape(
            groups, rows, tile_width - side
        )
        summed[a] = inside.reshape(groups, rows, tile_width)
        depart(a, 1)

    def send(a):
        spill(a).wait_recv()

        def body(g, carry):
            left = summed[a, g, :, :side] + spill_in[a, g].astype(f32)
            summed[a, g, :, :side] = left
            rounded[a, g, :, :side] = left.astype(bf16)
            return carry

        lax.fori_loop(0, groups, body, 0, unroll=2)
        for c in range(2):
            store(a, c).start()
        depart(a, 0)
        keep(a).start()

    def angle_step(a, carry):
        compute(a)
        return carry

    lax.fori_loop(0, angles, angle_step, 0)
    send(angles - 1)
    for a in range(angles):
        halo(a).wait_send()
        spill(a).wait_send()
        keep(a).wait()
        for c in range(2):
            store(a, c).wait()

    def finish(step, carry):
        for a in range(angles):
            for h in range(2):
                outgoing(a, h, step).wait_send()
                incoming(a, h, step).wait_recv()
        return carry

    lax.fori_loop(0, groups - 1, finish, 0)


def exit_gradient(starts, counts, own, probe, amp, fwd, inv):
    groups, angles, rows, tile_width = own.shape
    side = probe.shape[1]
    slots = starts.shape[1]
    n = groups * rows
    smem = pl.BlockSpec(memory_space=pltpu.SMEM)
    vmem = pl.BlockSpec(memory_space=pltpu.VMEM)
    hbm = pl.BlockSpec(memory_space=pl.ANY)
    dma = pltpu.SemaphoreType.DMA
    return pl.pallas_call(
        functools.partial(exit_kernel, slots=slots, groups=groups, angles=angles),
        name="exit_gradient",
        in_specs=[smem, smem, hbm, vmem, vmem, vmem, vmem],
        out_specs=[hbm, hbm],
        out_shape=[
            jax.ShapeDtypeStruct((2, groups, rows // 2, angles, tile_width), f32),
            jax.ShapeDtypeStruct((groups, angles, rows, tile_width), bf16),
        ],
        scratch_shapes=[
            pltpu.VMEM((angles, groups, rows, tile_width + side), bf16),
            pltpu.VMEM(((tile_width + side) // 128, n, 128), bf16),
            pltpu.VMEM((angles, groups, rows, tile_width), f32),
            pltpu.VMEM((angles, groups, rows, tile_width), bf16),
            pltpu.VMEM((n, slots * side), bf16),
            pltpu.VMEM((angles, groups, rows, side), bf16),
            pltpu.VMEM((angles, groups, rows, side), bf16),
            dma((angles,)),
            dma((angles, 2)),
            dma((angles,)),
            dma((2, angles)),
            dma((2, angles)),
            dma((angles, 2, groups - 1)),
            dma((angles, 2, groups - 1)),
        ],
        compiler_params=pltpu.CompilerParams(collective_id=2, has_side_effects=True),
    )(starts, counts, own, probe, amp, fwd, inv)


def back_kernel(ids, grad, tiles, exact, out, kept, *scratch, feeds, pairs, angles):
    step = pl.program_id(0)
    accs = scratch[:-2]
    held, sem = scratch[-2:]
    steps = pl.num_programs(0)
    total = steps * angles
    take = pltpu.make_async_copy(exact, held, sem.at[0])
    give = pltpu.make_async_copy(held, kept, sem.at[1])

    @pl.when(step == 0)
    def _():
        take.start()

    @pl.when(step == steps // 2)
    def _():
        take.wait()
        give.start()

    owners, rows, width = out.shape
    blocks = accs[0].shape[0]

    @pl.when(step == 0)
    def _():
        def clear(i, carry):
            for acc in accs:
                acc[pl.ds(i * 8, 8)] = jnp.zeros((8, rows, 128), f32)
            return carry

        lax.fori_loop(0, blocks // 8, clear, 0)

    half = pairs * rows
    lo = low_half((half, 128))
    for a in range(angles):
        at = step * angles + a
        flat = jnp.concatenate(
            [grad[0, a, :, bp * 128 : (bp + 1) * 128] for bp in range(pairs)], axis=0
        )
        zero = jnp.zeros_like(flat)
        halves = jnp.concatenate([jnp.where(lo, flat, zero), jnp.where(lo, zero, flat)], axis=0)
        twice = jnp.concatenate([tiles[a], tiles[a]], axis=0)
        contrib = jnp.dot(halves, twice, preferred_element_type=f32)
        for parity in range(2):
            for bp in range(pairs):
                first = (2 * bp + parity) * feeds
                top = (parity * pairs + bp) * rows
                where = [ids[(first + j) * total + at] for j in range(feeds)]
                old = [accs[j][where[j]] for j in range(feeds)]
                for j in range(feeds):
                    lane = j // 2 * 128
                    accs[j][where[j]] = old[j] + contrib[top : top + rows, lane : lane + 128]

    @pl.when(step == steps - 1)
    def _():
        give.wait()
        lo = low_half((rows, 128))
        per_owner = width // 128

        def join(p, carry):
            at = pl.multiple_of(p * 128, 128)
            for o in range(owners):
                kb = 2 * (o * per_owner + p)
                even_lo = sum(accs[j][kb] for j in range(0, feeds, 2))
                even_hi = sum(accs[j][kb] for j in range(1, feeds, 2))
                odd_lo = sum(accs[j][kb + 1] for j in range(0, feeds, 2))
                odd_hi = sum(accs[j][kb + 1] for j in range(1, feeds, 2))
                joined = jnp.where(lo, even_lo, odd_hi) + pltpu.roll(
                    jnp.where(lo, odd_lo, even_hi), 64, 1
                )
                out[o, :, pl.ds(at, 128)] = joined.astype(bf16)
            return carry

        lax.fori_loop(0, per_owner, join, 0, unroll=2)


def back_project(ids, grad, tiles, exact, owners, coefs):
    groups, angles, rows, tile_width = grad.shape
    angle_count, block, span = tiles.shape
    feeds = span // block
    dets = tile_width // block
    blocks = coefs // block
    width = coefs // owners
    return pl.pallas_call(
        functools.partial(back_kernel, feeds=feeds, pairs=dets // 2, angles=angles),
        name="back_project",
        out_shape=[
            jax.ShapeDtypeStruct((owners, rows, width), bf16),
            jax.ShapeDtypeStruct(exact.shape, f32),
        ],
        grid_spec=pltpu.PrefetchScalarGridSpec(
            num_scalar_prefetch=1,
            grid=(groups,),
            in_specs=[
                pl.BlockSpec((1, angles, rows, tile_width), lambda g, ids: (g, 0, 0, 0)),
                pl.BlockSpec((angles, block, span), lambda g, ids: (g, 0, 0)),
                pl.BlockSpec(memory_space=pl.ANY),
            ],
            out_specs=[
                pl.BlockSpec((owners, rows, width), lambda g, ids: (0, 0, 0)),
                pl.BlockSpec(memory_space=pl.ANY),
            ],
            scratch_shapes=[pltpu.VMEM((blocks, rows, 128), f32) for _ in range(feeds)]
            + [pltpu.VMEM(exact.shape, f32), pltpu.SemaphoreType.DMA((2,))],
        ),
    )(ids, grad, tiles, exact)


def reduce_kernel(share, vol, out, near, mixed, far, send, recv):
    rows, width = vol.shape
    pos, partner, cross = pos_peers()
    beyond = lax.rem(partner + 2, 4)
    barrier = pltpu.get_barrier_semaphore()
    pl.semaphore_signal(barrier, inc=1, device_id={"pos": partner}, device_id_type=MESH)
    pl.semaphore_signal(barrier, inc=1, device_id={"pos": cross}, device_id_type=MESH)
    pl.semaphore_wait(barrier, 2)

    pieces = 4
    piece = width // pieces
    chunk = 512

    def columns(k):
        return pl.ds(k * piece, piece)

    def side(k):
        return remote(
            share.at[beyond, :, columns(k)], near.at[0, :, columns(k)], send.at[k], recv.at[k],
            {"pos": partner},
        )

    def over(k):
        return remote(
            mixed.at[:, columns(k)], far.at[:, columns(k)], send.at[pieces + k],
            recv.at[pieces + k], {"pos": cross},
        )

    home = remote(
        share.at[partner], near.at[1], send.at[2 * pieces], recv.at[2 * pieces], {"pos": partner}
    )
    for k in range(pieces):
        side(k).start()
    home.start()

    def mix(k):
        def body(i, carry):
            at = pl.ds(pl.multiple_of(k * piece + i * chunk, chunk), chunk)
            both = share[cross, :, at].astype(f32) + near[0, :, at].astype(f32)
            mixed[:, at] = both.astype(bf16)
            return carry

        lax.fori_loop(0, piece // chunk, body, 0)

    def total(k):
        def body(i, carry):
            at = pl.ds(pl.multiple_of(k * piece + i * chunk, chunk), chunk)
            both = share[pos, :, at].astype(f32) + near[1, :, at].astype(f32)
            out[:, at] = vol[:, at].astype(f32) + step_size * (both + far[:, at].astype(f32))
            return carry

        lax.fori_loop(0, piece // chunk, body, 0)

    for k in range(pieces):
        side(k).wait_recv()
        mix(k)
        if k > 0:
            over(k - 1).start()
    home.wait_recv()
    over(pieces - 1).start()
    for k in range(pieces):
        over(k).wait_recv()
        total(k)
    for k in range(pieces):
        side(k).wait_send()
        over(k).wait_send()
    home.wait_send()


def reduce_step(share, vol):
    rows, width = vol.shape
    vmem = pl.BlockSpec(memory_space=pltpu.VMEM)
    dma = pltpu.SemaphoreType.DMA
    return pl.pallas_call(
        reduce_kernel,
        name="reduce_step",
        out_shape=jax.ShapeDtypeStruct((rows, width), f32),
        in_specs=[vmem, vmem],
        out_specs=vmem,
        scratch_shapes=[
            pltpu.VMEM((2, rows, width), bf16),
            pltpu.VMEM((rows, width), bf16),
            pltpu.VMEM((rows, width), bf16),
            dma((9,)),
            dma((9,)),
        ],
        compiler_params=pltpu.CompilerParams(collective_id=1, has_side_effects=True),
    )(share, vol)


def on_device(volume, radon_tiles, tile_blocks, probe_field, amplitudes, offsets, counts):
    n_pos = lax.axis_size("pos")
    n_ang = lax.axis_size("ang")
    pos_index = lax.axis_index("pos")
    parts, slab, width = volume.shape
    block = radon_tiles.shape[1]
    own_blocks = tile_blocks.shape[1] // n_pos
    tile_width = own_blocks * block
    side = probe_field.shape[1]
    angles = amplitudes.shape[0]
    rows = parts * slab

    held = volume.reshape(rows, width)
    by_angle = tile_blocks.transpose(1, 2, 0)
    ids = lax.dynamic_slice_in_dim(by_angle, pos_index * own_blocks, own_blocks, 0).reshape(-1)
    fwd, inv = dft_tables(side)
    own = project(ids, held, radon_tiles, n_ang, n_pos)
    grad, back = exit_gradient(offsets, counts.reshape(-1), own, probe_field, amplitudes, fwd, inv)
    share, kept = back_project(ids, back, radon_tiles, grad, n_pos, n_pos * width)
    new_volume = reduce_step(share, held).reshape(volume.shape)
    proj_grad = kept.reshape(parts, n_ang * slab, angles, tile_width)
    return (new_volume, proj_grad)


def solution(mesh):
    in_specs = (
        P(None, "ang", "pos"),
        P(),
        P(),
        P(),
        P("ang", "pos", None, None),
        P("ang", "pos"),
        P("ang", "pos"),
    )
    out_specs = (P(None, "ang", "pos"), P(None, None, "ang", "pos"))
    return jax.shard_map(
        on_device, mesh=mesh, in_specs=in_specs, out_specs=out_specs, check_vma=False
    )
```
